512 devices in a mesh: energy: 64 (over z, x, core), slab: 8 (over y).
Axes of the slice: x: 4, y: 8, z: 8, core: 2. Of those that a mesh axis runs over, the one named last changes fastest.
Arguments:
- energies: float32 [64], P('energy'), may hold values from 0.6 to 1.2
- hamiltonian: float32 [8, 256, 256], P('slab')
- coupling: float32 [8, 64, 64], P('slab'), may hold values from -1.04 to 1.04
- green_prev: float32 [64, 8, 2, 256, 256], P('energy', 'slab'), may hold values from -0.5 to 0.5
- profile: float32 [256, 256], replicated, may hold values from 0.2 to 1
- phonon_weights: float32 [8], replicated, may hold values from 0.02 to 0.1
- source: int32 [64, 2], P('energy'), may hold values from 0 to 63, as said below
- weight_index: int32 [64, 2], P('energy'), may hold values from 0 to 7
- left_face: int32 [8, 64], P('slab'), may hold values from 0 to 255, as said below
- right_face: int32 [8, 64], P('slab'), may hold values from 0 to 255, as said below
Outputs:
- green: float32 [64, 8, 2, 256, 256], P('energy', 'slab')
The draws below stay inside these ranges and needn't reach their ends.
Inputs may be any that keep to these rules, and one draw needn't show every extreme that they name: source[j, 0] = min(j + d, 63) and source[j, 1] = max(j - d', 0) with d, d' in 1 .. 5; in each column some energy has its partner exactly 5 points away. `left_face`: each row holds 64 distinct orbitals. right_face[s] holds the same 64 orbitals as left_face[s], in an order of its own.
All inputs are finite; a program needn't handle non-finite values.
Results may differ from the reference program's by a relative error of at most 0.00011.
Values sent between devices are 32-bit elements; how exact they have to be, the bound alone decides.
A program may use at most 64 MiB of HBM per device.

```python
import math
import jax
import jax.numpy as jnp
from jax import lax

W = 256
S = 64
SPAN = 5
NW = 8
NEWTON = 5
NE = 64
SLABS = 8


def draw_hamiltonian(key, part):
    key_a, key_b = jax.random.split(jax.random.fold_in(key, 5))
    raw = jax.random.normal(key_a, (SLABS, W, W), jnp.float32)
    onsite = jax.random.uniform(key_b, (SLABS, W), jnp.float32, -0.1, 0.1)
    scaled = raw * (0.1 * (2.0 / W) ** 0.5)
    symmetric = 0.5 * (scaled + jnp.swapaxes(scaled, 1, 2))
    return symmetric + onsite[:, :, None] * jnp.eye(W, dtype=jnp.float32)[None]


def draw_coupling(key, part):
    key_size, key_sign, key_noise = jax.random.split(jax.random.fold_in(key, 53), 3)
    signs = jnp.where(jax.random.bernoulli(key_sign, 0.5, (SLABS, S)), 1.0, -1.0).astype(jnp.float32)
    size = jax.random.uniform(key_size, (SLABS, S), jnp.float32, 0.75, 1.25)
    noise = jnp.clip(jax.random.normal(key_noise, (SLABS, S, S), jnp.float32), -3.0, 3.0)
    unit = jnp.eye(S, dtype=jnp.float32)
    off_part = noise * (1.0 - unit)[None] * (0.8 * 0.25 / S ** 0.5)
    return 0.8 * (signs * size)[:, :, None] * unit[None] + off_part


def draw_source(key, part):
    key_off, key_pos = jax.random.split(jax.random.fold_in(key, 11))
    offsets = jax.random.randint(key_off, (NE, 2), 1, SPAN + 1)
    spots = jax.random.randint(key_pos, (2,), SPAN, NE - SPAN)
    offsets = offsets.at[spots, jnp.arange(2)].set(SPAN)
    points = jnp.arange(NE, dtype=jnp.int32)
    upper = jnp.minimum(points + offsets[:, 0], NE - 1)
    lower = jnp.maximum(points - offsets[:, 1], 0)
    return jnp.stack([upper, lower], axis=1).astype(jnp.int32)


def face_indices(key):
    keys = jax.random.split(jax.random.fold_in(key, 21), SLABS)
    return jax.vmap(lambda item: jax.random.permutation(item, W)[:S])(keys).astype(jnp.int32)


def draw_left_face(key, part):
    return face_indices(key)


def draw_right_face(key, part):
    left = face_indices(key)
    keys = jax.random.split(jax.random.fold_in(key, 37), SLABS)
    order = jax.vmap(lambda item: jax.random.permutation(item, S))(keys).astype(jnp.int32)
    return jnp.take_along_axis(left, order, axis=1).astype(jnp.int32)


def place_ends(entries, key, least, largest):
    spot = [jax.random.randint(jax.random.fold_in(key, axis), (), 0, length) for axis, length in enumerate(entries.shape)]
    main_axis = entries.shape.index(max(entries.shape))
    next_to = spot[:main_axis] + [(spot[main_axis] + 1) % entries.shape[main_axis]] + spot[main_axis + 1:]
    return entries.at[tuple(spot)].set(least).at[tuple(next_to)].set(largest)


def levels(own_key, extent, shards, smallest, high):
    def one(position, blocks):
        draws = jax.random.uniform(jax.random.fold_in(jax.random.fold_in(own_key, 6), position), (blocks,), jnp.float32, smallest / len(shards), high / len(shards))
        return jnp.repeat(jnp.exp(draws), extent[position] // blocks).reshape((-1,) + (1,) * (len(extent) - position - 1))

    loudness = one(*shards[0])
    for cut in shards[1:]:
        loudness = loudness * one(*cut)
    return loudness


def bell_draw(own_key, shape, spread, bound, pieces=(), kind=jnp.bfloat16):
    entries = spread * jax.random.normal(own_key, shape, jnp.float32)
    if pieces:
        entries = entries * levels(own_key, shape, pieces, -0.22, 0.18)
    return jnp.clip(entries, -bound, bound).astype(kind)


def setup_inputs(seed: int = 0) -> dict:
    splits = jax.random.split(jax.random.key(seed), 11)
    return {
        "energies": jnp.clip(0.6 + 0.6 * jax.random.uniform(splits[0], (NE,), jnp.float32) ** levels(splits[0], (NE,), ((0, 64),), -0.2, 0.2), 0.6, 1.2),
        "hamiltonian": draw_hamiltonian(jax.random.fold_in(splits[10], 71), 0),
        "coupling": draw_coupling(jax.random.fold_in(splits[10], 71), 0),
        "green_prev": bell_draw(splits[3], (NE, SLABS, 2, W, W), (0.5 / W ** 0.5), 0.5, ((0, 64), (1, 8)), jnp.float32),
        "profile": jnp.clip(jax.random.uniform(splits[4], (W, W), jnp.float32, 0.2, 1.0), 0.2, 1.0),
        "phonon_weights": jnp.clip(jnp.exp(jax.random.uniform(splits[5], (NW,), jnp.float32, math.log(0.02), math.log(0.1))), 0.02, 0.1),
        "source": draw_source(jax.random.fold_in(splits[10], 71), 0),
        "weight_index": place_ends(jax.random.randint(splits[7], (NE, 2), 0, NW), jax.random.fold_in(splits[7], 1), 0, NW - 1).astype(jnp.int32),
        "left_face": draw_left_face(jax.random.fold_in(splits[10], 71), 0),
        "right_face": draw_right_face(jax.random.fold_in(splits[10], 71), 0),
    }


BROAD = 0.02
highest = lax.Precision.HIGHEST

def product(left, right):
    return jnp.matmul(left, right, precision=highest)

def complex_product(a_real, a_imag, b_real, b_imag):
    return (product(a_real, b_real) - product(a_imag, b_imag), product(a_real, b_imag) + product(a_imag, b_real))

def invert(a_real, a_imag):
    width = a_real.shape[-1]
    unit = jnp.eye(width, dtype=a_real.dtype)
    modulus = jnp.sqrt(a_real * a_real + a_imag * a_imag)
    col_norm = lax.optimization_barrier(jnp.max(lax.optimization_barrier(jnp.sum(modulus, axis=-2)), axis=-1))
    row_norm = lax.optimization_barrier(jnp.max(lax.optimization_barrier(jnp.sum(modulus, axis=-1)), axis=-1))
    scale = (1.0 / (col_norm * row_norm))[..., None, None]
    x_real = scale * jnp.swapaxes(a_real, -1, -2)
    x_imag = -scale * jnp.swapaxes(a_imag, -1, -2)
    for turn in range(NEWTON):
        p_real, p_imag = complex_product(a_real, a_imag, x_real, x_imag)
        x_real, x_imag = complex_product(x_real, x_imag, 2.0 * unit - p_real, -p_imag)
    return (x_real, x_imag)

def reference(energies, hamiltonian, coupling, green_prev, profile, phonon_weights, source, weight_index, left_face, right_face):
    width = hamiltonian.shape[1]
    unit = jnp.eye(width, dtype=hamiltonian.dtype)
    firsts = jnp.arange(SLABS) == 0

    def one_energy(items):
        energy, src, widx = items
        picked = green_prev[src]
        weights = phonon_weights[widx]
        sigma = profile * (weights[0] * picked[0] + weights[1] * picked[1])

        def forward(carry, slab):
            face_real, face_imag = carry
            ham, coup, sig, left, right, first = slab
            lead = -0.5 * product(coup.T, coup)
            inner_real = product(product(coup.T, face_real), coup)
            inner_imag = product(product(coup.T, face_imag), coup)
            b_real = jnp.where(first, 0.0, inner_real)
            b_imag = jnp.where(first, lead, inner_imag)
            a_real = energy * unit - ham - sig[0]
            a_imag = BROAD * unit - sig[1]
            a_real = a_real.at[left[:, None], left[None, :]].add(-b_real)
            a_imag = a_imag.at[left[:, None], left[None, :]].add(-b_imag)
            g_real, g_imag = invert(a_real, a_imag)
            out = (g_real[right][:, right], g_imag[right][:, right])
            return (out, (g_real, g_imag))
        zeros = jnp.zeros((S, S), hamiltonian.dtype)
        carry, (g_real, g_imag) = lax.scan(forward, (zeros, zeros), (hamiltonian, coupling, sigma, left_face, right_face, firsts))

        def backward(carry, slab):
            m_real, m_imag = carry
            gr_one, gi_one, coup, left, right = slab
            t_real, t_imag = complex_product(gr_one[:, right], gi_one[:, right], m_real, m_imag)
            c_real, c_imag = complex_product(t_real, t_imag, gr_one[right], gi_one[right])
            big_real = gr_one + c_real
            big_imag = gi_one + c_imag
            corner_real = big_real[left][:, left]
            corner_imag = big_imag[left][:, left]
            out = (product(product(coup, corner_real), coup.T), product(product(coup, corner_imag), coup.T))
            return (out, jnp.stack([big_real, big_imag], axis=0))
        carry, blocks = lax.scan(backward, (zeros, zeros), (g_real, g_imag, coupling, left_face, right_face), reverse=True)
        return blocks
    return lax.map(one_energy, (energies, source, weight_index))
```

```python
import functools
import jax
import jax.numpy as jnp
from jax import lax
from jax.experimental import pallas as pl
from jax.experimental.pallas import tpu as pltpu
from jax.sharding import PartitionSpec as P

SPAN = 5
BROAD = 0.02
f32 = jnp.float32
bf16 = jnp.bfloat16
MESH = pl.DeviceIdType.MESH
highest = lax.Precision.HIGHEST


def mm(left, right):
    return jnp.dot(left, right, preferred_element_type=f32)


def mmt(left, right):
    return lax.dot_general(left, right, (((1,), (1,)), ((), ())), preferred_element_type=f32)


def split(value):
    high = value.astype(bf16)
    return high, (value - high.astype(f32)).astype(bf16)


def lanes(*pieces):
    return jnp.concatenate(pieces, axis=1)


def rows(*pieces):
    return jnp.concatenate(pieces, axis=0)


def left3(value):
    high, low = split(value)
    return lanes(high, high, low)


def right3(value):
    high, low = split(value)
    return lanes(high, low, high)


def right3v(value):
    high, low = split(value)
    return rows(high, low, high)


def swapped(packed, low_sign, high_sign):
    half = packed.shape[1] // 2
    lane = lax.broadcasted_iota(jnp.int32, packed.shape, 1)
    turned = lanes(packed[:, half:], packed[:, :half])
    return jnp.where(lane < half, low_sign * turned, high_sign * turned)


def as_right(packed):
    return rows(packed, swapped(packed, -1.0, 1.0))


def chain_kernel(
    slabs, width, faces,
    a0r_ref, a0i_ref, perm_ref, perm_t_ref, ends_ref, d_ref, lead_ref,
    out_ref,
    sk_ref, lhs_ref, w_ref, a_ref, b_ref, m_ref, send_ref, send_back_ref, pa_ref, x_ref, colrow_ref,
    send_sem, recv_sem,
):
    slab = lax.axis_index("slab")
    F = faces
    barrier = pltpu.get_barrier_semaphore()
    for step in (1, slabs - 1):
        pl.semaphore_signal(
            barrier, inc=1, device_id={"slab": lax.rem(slab + step, slabs)}, device_id_type=MESH
        )

    perm = perm_ref[...]
    pieces = split(a0r_ref[...]) + split(a0i_ref[...])
    turned = mmt(rows(*pieces), perm).astype(bf16)
    placed = mm(perm, lanes(*[turned[k * width:(k + 1) * width] for k in range(4)]))
    a_real = placed[:, :width] + placed[:, width:2 * width]
    a_imag = placed[:, 2 * width:3 * width] + placed[:, 3 * width:]
    a_ref[:, :width] = a_real
    a_ref[:, width:] = a_imag
    row = lax.broadcasted_iota(jnp.int32, (width, width), 0)
    col = lax.broadcasted_iota(jnp.int32, (width, width), 1)
    inner = (row < F) & (col < F)
    unit = jnp.where(row == col, 1.0, 0.0)
    modulus = jnp.where(inner, 0.0, jnp.sqrt(a_real * a_real + a_imag * a_imag))
    row_sums = jnp.sum(modulus, axis=1, keepdims=True)
    col_sums = jnp.sum(modulus, axis=0, keepdims=True)
    pa_ref[...] = lanes(a_real[:, :F], a_imag[:, :F])
    open_real = jnp.where(inner, 0.0, a_real)
    open_imag = jnp.where(inner, 0.0, a_imag)
    rh, rl = split(open_real)
    ih, il = split(open_imag)
    left = rows(lanes(rh, rh, rl, ih, ih, il), lanes(ih, ih, il, -rh, -rh, -rl))
    sk_ref[...] = mmt(left, lanes(rh, rl, rh, ih, il, ih))

    @pl.when(slab == 0)
    def _():
        b_ref[...] = lanes(jnp.zeros((F, F), f32), lead_ref[...])

    pl.semaphore_wait(barrier, 2)

    def hand_on(source, target, device, sems):
        return pltpu.make_async_remote_copy(
            src_ref=source, dst_ref=target, send_sem=send_sem.at[sems], recv_sem=recv_sem.at[sems],
            device_id={"slab": device}, device_id_type=MESH,
        )

    forward = hand_on(send_ref, b_ref, lax.rem(slab + 1, slabs), 0)
    backward = hand_on(send_back_ref, m_ref, lax.rem(slab + slabs - 1, slabs), 1)

    @pl.when(slab > 0)
    def _():
        forward.wait_recv()

    face = pa_ref[:F, :] - b_ref[...]
    pa_ref[:F, :] = face
    square = face * face
    face_mod = jnp.sqrt(square[:, :F] + square[:, F:])
    face_rows = jnp.sum(face_mod, axis=1, keepdims=True) + row_sums[:F]
    face_cols = jnp.sum(face_mod, axis=0, keepdims=True) + col_sums[:, :F]
    row_norm = jnp.maximum(jnp.max(row_sums[F:], axis=0, keepdims=True), jnp.max(face_rows, axis=0, keepdims=True))
    col_norm = jnp.maximum(jnp.max(col_sums[:, F:], axis=1, keepdims=True), jnp.max(face_cols, axis=1, keepdims=True))
    scale = 1.0 / (row_norm * col_norm)
    pa = pa_ref[...]
    other = swapped(face, 1.0, -1.0)
    ends = ends_ref[...]
    zero = jnp.zeros((F, F), f32)
    first = rows(face, other, lanes(ends, zero), lanes(zero, -ends))
    over = mmt(left3(first), right3(pa))
    down = mmt(left3(pa), right3(rows(face, -other)))
    inside = lax.broadcasted_iota(jnp.int32, (width, 2 * F), 1) < F
    below = (lax.broadcasted_iota(jnp.int32, (width, 2 * F), 0) >= F) & inside
    for part in range(2):
        base = part * width
        sk_ref[base:base + F, :] += over[part * F:(part + 1) * F]
        column = down if part == 0 else lanes(down[:, F:], down[:, :F])
        sk_ref[base:base + width, :2 * F] += jnp.where(below, column, 0.0)
    sym = unit - scale * sk_ref[:width, :]
    skew = -scale * sk_ref[width:, :]
    lr = scale * over[2 * F:3 * F]
    li = scale * over[3 * F:]

    def thin(real, imag):
        return lanes(left3(rows(real, imag)), left3(rows(-imag, real)))

    for level in range(3):
        w_ref[level, :, :] = rows(right3v(sym), right3v(skew))
        lhs_ref[level, :width, :] = lanes(left3(sym + skew), left3(sym - skew))
        lhs_ref[level, width:, :] = thin(lr, li)
        result = mm(lhs_ref[level], w_ref[level])
        grown = result[:width]
        flipped = grown.T
        sym = 0.5 * (grown + flipped)
        skew = 0.5 * (grown - flipped)
        lr = lr + result[width:width + F]
        li = li + result[width + F:]
    w_ref[3, :, :] = rows(right3v(sym), right3v(skew))
    ur, ui = sym[:F], skew[:F]
    result = mm(
        lanes(left3(rows(lr, li, ur, ui)), left3(rows(-li, lr, -ui, ur))), w_ref[3]
    )
    w1r, w1i = ur + unit[:F], ui
    w2r, w2i = ur + result[2 * F:3 * F], ui + result[3 * F:]
    left = left3(lanes(lr, li, result[:F], result[F:2 * F]))
    right = right3(rows(lanes(w1r, w1i, w2r, w2i), lanes(-w1i, w1r, -w2i, w2r)))
    packed = mmt(left, right)
    both = rows(lanes(ends, zero), lanes(zero, ends))
    packed = mmt(left3(packed), right3(both))

    @pl.when(slab < slabs - 1)
    def _():
        send_ref[...] = packed
        forward.start()

    @pl.when(slab == slabs - 1)
    def _():
        send_back_ref[...] = packed
        backward.start()

    lhs_ref[3, :width, :] = lanes(left3(sym + skew), left3(sym - skew))
    first_g = lhs_ref[0, :width, :]
    part_g = first_g[:, :width].astype(f32) + first_g[:, 2 * width:3 * width].astype(f32) + unit
    part_t = first_g[:, 3 * width:4 * width].astype(f32) + first_g[:, 5 * width:].astype(f32) + unit
    for level in range(1, 4):
        part_g = part_g + mm(lanes(left3(part_g), left3(part_t)), w_ref[level])
        part_t = part_g.T
    grown = mm(lhs_ref[3, :width, :], w_ref[3])
    flipped = grown.T
    last = rows(right3v(0.5 * (grown + flipped)), right3v(0.5 * (grown - flipped)))
    part_g = part_g + mm(lanes(left3(part_g), left3(part_t)), last)
    part_t = part_g.T
    pr = 0.5 * (part_g + part_t)
    pi = 0.5 * (part_g - part_t)
    a_ref[:F, :F] = face[:, :F]
    a_ref[:F, width:width + F] = face[:, F:]
    left = lanes(left3(a_ref[:, :width].T), left3(a_ref[:, width:].T))
    right = rows(right3v(lanes(pr, pi)), right3v(lanes(pi, -pr)))
    block = scale * mm(left, right)
    block_face = lanes(block[:F, :F], block[:F, width:width + F])
    hr, qr = split(block[:, :width])
    hi, qi = split(block[:, width:])
    turned = mm(perm_t_ref[...], lanes(hr, qr, hi, qi))
    back = turned.astype(bf16)
    back = mm(rows(*[back[:, k * width:(k + 1) * width] for k in range(4)]), perm)
    x_ref[0] = back[:width] + back[width:2 * width]
    x_ref[1] = back[2 * width:3 * width] + back[3 * width:]

    @pl.when(slab == slabs - 1)
    def _():
        out_ref[0, 0, :, :, :] = x_ref[...]

    @pl.when(slab < slabs - 1)
    def _():
        column = left3(
            lanes(
                turned[:, :F] + turned[:, width:width + F],
                turned[:, 2 * width:2 * width + F] + turned[:, 3 * width:3 * width + F],
            )
        )
        face_rows = mm(rows(hr[:F], qr[:F], hi[:F], qi[:F]), perm)
        rr = face_rows[:F] + face_rows[F:2 * F]
        ri = face_rows[2 * F:3 * F] + face_rows[3 * F:]
        across = right3v(rows(lanes(rr, ri), lanes(-ri, rr)))
        d = d_ref[...]
        d_both = right3(rows(lanes(d, zero), lanes(zero, d)))
        u = left3(mm(left3(d), right3v(block_face)))
        v = right3v(as_right(mmt(left3(block_face), d_both)))
        k = mmt(u, d_both)
        backward.wait_recv()
        incoming = right3v(as_right(m_ref[...]))

        @pl.when(slab > 0)
        def _():
            send_back_ref[...] = k + mm(left3(mm(u, incoming)), v)
            backward.start()

        more = mm(left3(mm(column, incoming)), across)
        out_ref[0, 0, 0, :, :] = x_ref[0] + more[:, :width]
        out_ref[0, 0, 1, :, :] = x_ref[1] + more[:, width:]

    @pl.when(slab < slabs - 1)
    def _():
        forward.wait_send()

    @pl.when(slab > 0)
    def _():
        backward.wait_send()


def run_chain(a0r, a0i, perm, ends, d_prev, lead):
    width, faces = a0r.shape[-1], ends.shape[0]
    slabs = lax.axis_size("slab")
    vmem = pl.BlockSpec(memory_space=pltpu.VMEM)
    return pl.pallas_call(
        functools.partial(chain_kernel, slabs, width, faces),
        out_shape=jax.ShapeDtypeStruct((1, 1, 2, width, width), f32),
        in_specs=[vmem] * 7,
        out_specs=vmem,
        scratch_shapes=[
            pltpu.VMEM((2 * width, width), f32),
            pltpu.VMEM((4, width + 2 * faces, 6 * width), bf16),
            pltpu.VMEM((4, 6 * width, width), bf16),
            pltpu.VMEM((width, 2 * width), f32),
            pltpu.VMEM((faces, 2 * faces), f32),
            pltpu.VMEM((faces, 2 * faces), f32),
            pltpu.VMEM((faces, 2 * faces), f32),
            pltpu.VMEM((faces, 2 * faces), f32),
            pltpu.VMEM((width, 2 * faces), f32),
            pltpu.VMEM((2, width, width), f32),
            pltpu.VMEM((8, 128), f32),
            pltpu.SemaphoreType.DMA((2,)),
            pltpu.SemaphoreType.DMA((2,)),
        ],
        compiler_params=pltpu.CompilerParams(collective_id=0, has_side_effects=True),
        name="chain",
    )(a0r, a0i, perm, perm.T, ends, d_prev, lead)


def passed_along(value, axis, steps):
    count = lax.axis_size(axis)
    initial, last = (max(0, -steps), min(count, count - steps))
    return lax.ppermute(value, axis, [(source, source + steps) for source in range(initial, last)])


def product(left, right):
    return jnp.matmul(left, right, precision=highest)


def on_device(
    energies, hamiltonian, coupling, green_prev, profile, phonon_weights, source, weight_index, left_face, right_face,
):
    width = hamiltonian.shape[1]
    base = lax.axis_index("energy")
    table_size = phonon_weights.shape[0]
    chosen = jnp.sum(
        phonon_weights[None, :] * (weight_index[0][:, None] == jnp.arange(table_size, dtype=jnp.int32)[None, :]),
        axis=1,
    )
    own = green_prev[0, 0]

    def coef(position):
        return jnp.sum(chosen * (source[0] == position))

    summed = coef(base) * own
    for offset in range(1, SPAN + 1):
        summed = summed + coef(base + offset) * passed_along(own, "energy", -offset)
        summed = summed + coef(base - offset) * passed_along(own, "energy", offset)
    sigma = summed * profile
    unit = jnp.eye(width, dtype=f32)
    a_real = energies[0] * unit - hamiltonian[0] - sigma[0]
    a_imag = BROAD * unit - sigma[1]
    return chain_part(a_real, a_imag, coupling, left_face, right_face)


def chain_part(a_real, a_imag, coupling, left_face, right_face):
    width = a_real.shape[0]
    coup = coupling[0]
    orbitals = jnp.arange(width, dtype=jnp.int32)
    left, right = left_face[0], right_face[0]
    faces = left.shape[0]
    slab, slabs = lax.axis_index("slab"), lax.axis_size("slab")
    hot = left[:, None] == orbitals[None, :]
    on_face = jnp.any(hot, axis=0)
    place = jnp.sum(jnp.where(hot, jnp.arange(faces, dtype=jnp.int32)[:, None], 0), axis=0)
    before = jnp.sum(((orbitals[:, None] < orbitals[None, :]) & ~on_face[:, None]).astype(jnp.int32), axis=0)
    position = jnp.where(on_face, place, faces + before)
    perm = (orbitals[:, None] == position[None, :]).astype(bf16)
    order = (left[:, None] == right[None, :]).astype(f32)
    d_here = product(order, passed_along(coup, "slab", -1))
    d_prev = passed_along(d_here, "slab", 1)
    ends = jnp.where(slab < slabs - 1, d_here.T, d_prev)
    lead = -0.5 * product(coup.T, coup)
    return run_chain(a_real, a_imag, perm, ends, d_prev, lead)


def solution(mesh):
    in_specs = (
        P("energy"),
        P("slab", None, None),
        P("slab", None, None),
        P("energy", "slab", None, None, None),
        P(),
        P(),
        P("energy", None),
        P("energy", None),
        P("slab", None),
        P("slab", None),
    )
    out_specs = P("energy", "slab", None, None, None)
    return jax.shard_map(on_device, mesh=mesh, in_specs=in_specs, out_specs=out_specs, check_vma=False)
```

```python
import functools
import jax
import jax.numpy as jnp
from jax import lax
from jax.experimental import pallas as pl
from jax.experimental.pallas import tpu as pltpu
from jax.sharding import PartitionSpec as P

BROAD = 0.02
f32 = jnp.float32
bf16 = jnp.bfloat16
MESH = pl.DeviceIdType.MESH


def mm(left, right):
    return jnp.dot(left, right, preferred_element_type=f32)


def mmt(left, right):
    return lax.dot_general(left, right, (((1,), (1,)), ((), ())), preferred_element_type=f32)


def split(value):
    high = value.astype(bf16)
    return high, (value - high.astype(f32)).astype(bf16)


def lanes(*pieces):
    return jnp.concatenate(pieces, axis=1)


def rows(*pieces):
    return jnp.concatenate(pieces, axis=0)


def left3(value):
    high, low = split(value)
    return lanes(high, high, low)


def right3(value):
    high, low = split(value)
    return lanes(high, low, high)


def right3v(value):
    high, low = split(value)
    return rows(high, low, high)


def swapped(packed, low_sign, high_sign):
    half = packed.shape[1] // 2
    lane = lax.broadcasted_iota(jnp.int32, packed.shape, 1)
    turned = lanes(packed[:, half:], packed[:, :half])
    return jnp.where(lane < half, low_sign * turned, high_sign * turned)


def as_right(packed):
    return rows(packed, swapped(packed, -1.0, 1.0))


NX = 4
CORES = 2
CHUNKS = 16
AHEAD = 4
FAR_LAG = 2
PARTNER_LAG = 4
LINE_LAG = 6
TABLE = 32


def where_on_energy():
    spot = lax.axis_index("energy")
    core = lax.rem(spot, CORES)
    chip = lax.div(spot, CORES)
    return lax.rem(chip, NX), lax.div(chip, NX), core


def energy_of(x, z, core):
    return (z * NX + x) * CORES + core


def remote(source, target, send, recv, **device):
    return pltpu.make_async_remote_copy(
        src_ref=source, dst_ref=target, send_sem=send, recv_sem=recv, device_id=device, device_id_type=MESH
    )


def greet(lines, slabs):
    x, z, core = where_on_energy()
    barrier = pltpu.get_barrier_semaphore()

    def signal(**device):
        pl.semaphore_signal(barrier, inc=1, device_id=device, device_id_type=MESH)

    signal(energy=energy_of(lax.rem(x + 1, NX), z, core))
    signal(energy=energy_of(lax.rem(x + NX - 1, NX), z, core))
    signal(energy=energy_of(x, z, 1 - core))
    count = 3
    for step, there in ((1, z < lines - 1), (-1, z > 0)):
        @pl.when(there)
        def _():
            signal(energy=energy_of(x, z + step, core))
            signal(energy=energy_of(x, z + step, 1 - core))
        count = count + 2 * there.astype(jnp.int32)
    if slabs > 1:
        slab = lax.axis_index("slab")
        for step in (1, slabs - 1):
            signal(slab=lax.rem(slab + step, slabs))
        count = count + 2
    return barrier, count


def make_table(source_ref, index_ref, weights_ref, table_ref):
    here = lax.axis_index("energy")
    row = lax.broadcasted_iota(jnp.int32, (TABLE, 128), 0)
    total = jnp.zeros((TABLE, 128), f32)
    for term in range(2):
        weight = weights_ref[index_ref[0, term]]
        distance = source_ref[0, term] - here + TABLE // 2
        total = total + jnp.where(row == distance, weight, 0.0)
    table_ref[0] = total


def exchange(lines, own, table_ref, got, part_send, part_recv, line_send, line_recv, acc,
             send_sem, recv_sem, table_send, table_recv, meanwhile, finish):
    x, z, core = where_on_energy()
    depth = own.shape[0] // CHUNKS
    right = energy_of(lax.rem(x + 1, NX), z, core)
    left = energy_of(lax.rem(x + NX - 1, NX), z, core)
    partner = energy_of(x, z, 1 - core)
    up_there, down_there = z < lines - 1, z > 0
    up, down = energy_of(x, z + 1, core), energy_of(x, z - 1, core)
    up_other, down_other = energy_of(x, z + 1, 1 - core), energy_of(x, z - 1, 1 - core)

    def part(ref, chunk):
        return ref.at[pl.ds(chunk * depth, depth), :]

    def tables(flow, device):
        return remote(table_ref.at[0], table_ref.at[flow + 1], table_send.at[flow], table_recv.at[flow], energy=device)

    to_partner = tables(0, partner)
    to_up, to_up_other = tables(3, up), tables(4, up_other)
    to_down, to_down_other = tables(1, down), tables(2, down_other)

    def piece(flow, chunk, source, target, device):
        return remote(source, target, send_sem.at[flow, chunk], recv_sem.at[flow, chunk], energy=device)

    to_right = [piece(0, q, part(own, q), part(got.at[0], q), right) for q in range(CHUNKS)]
    to_left = [piece(1, q, part(own, q), part(got.at[1], q), left) for q in range(CHUNKS)]
    onward = [
        piece(2, q, part(got.at[q % 2], q), part(got.at[2], q), right if q % 2 == 0 else left)
        for q in range(CHUNKS)
    ]
    across = [
        [piece(3 + k, q, part(part_send.at[k], q), part(part_recv.at[k], q), partner) for q in range(CHUNKS)]
        for k in range(3)
    ]
    upward = [piece(6, q, part(line_send.at[0], q), part(line_recv.at[0], q), up) for q in range(CHUNKS)]
    downward = [piece(7, q, part(line_send.at[1], q), part(line_recv.at[1], q), down) for q in range(CHUNKS)]

    def own_start(chunk):
        to_right[chunk].start()
        to_left[chunk].start()

    for chunk in range(AHEAD):
        own_start(chunk)
    to_partner.start()

    @pl.when(up_there)
    def _():
        to_up.start()
        to_up_other.start()

    @pl.when(down_there)
    def _():
        to_down.start()
        to_down_other.start()

    meanwhile()
    to_partner.wait()

    @pl.when(up_there)
    def _():
        to_up.wait_send()
        to_up_other.wait_send()
        to_down.wait_recv()
        to_down_other.wait_recv()

    @pl.when(down_there)
    def _():
        to_down.wait_send()
        to_down_other.wait_send()
        to_up.wait_recv()
        to_up_other.wait_recv()

    apart = [0] + [lax.rem(x + step, NX) - x for step in (3, 1, 2)]

    def weighted(slot, line, other, chunk):
        total = None
        for k in range(4):
            lag = 2 * apart[k] + (2 * core - 1 if other else 0) - 8 * line + TABLE // 2
            weight = table_ref[slot, pl.ds(lag, 1), :]
            block = (own if k == 0 else got.at[k - 1])[pl.ds(chunk * depth, depth), :]
            term = lanes(weight, weight) * block
            total = term if total is None else total + term
        return total

    for step in range(CHUNKS + LINE_LAG):
        q = step
        if q < CHUNKS:
            to_right[q].wait_recv()
            to_left[q].wait_recv()
            onward[q].start()
            if q + AHEAD < CHUNKS:
                own_start(q + AHEAD)
        q = step - FAR_LAG
        if 0 <= q < CHUNKS:
            onward[q].wait_recv()
            piece_rows = pl.ds(q * depth, depth)
            acc[piece_rows, :] = weighted(0, 0, False, q)
            part_send[0, piece_rows, :] = weighted(1, 0, True, q)
            across[0][q].start()

            @pl.when(up_there)
            def _():
                line_send[0, piece_rows, :] = weighted(2, 1, False, q)
                part_send[1, piece_rows, :] = weighted(3, 1, True, q)
                across[1][q].start()

            @pl.when(down_there)
            def _():
                line_send[1, piece_rows, :] = weighted(4, -1, False, q)
                part_send[2, piece_rows, :] = weighted(5, -1, True, q)
                across[2][q].start()
        q = step - PARTNER_LAG
        if 0 <= q < CHUNKS:
            piece_rows = pl.ds(q * depth, depth)
            across[0][q].wait_recv()
            acc[piece_rows, :] += part_recv[0, piece_rows, :]

            @pl.when(up_there)
            def _():
                across[1][q].wait_recv()
                line_send[0, piece_rows, :] += part_recv[1, piece_rows, :]
                upward[q].start()

            @pl.when(down_there)
            def _():
                across[2][q].wait_recv()
                line_send[1, piece_rows, :] += part_recv[2, piece_rows, :]
                downward[q].start()
        q = step - LINE_LAG
        if 0 <= q < CHUNKS:
            piece_rows = pl.ds(q * depth, depth)

            @pl.when(down_there)
            def _():
                upward[q].wait_recv()
                acc[piece_rows, :] += line_recv[0, piece_rows, :]

            @pl.when(up_there)
            def _():
                downward[q].wait_recv()
                acc[piece_rows, :] += line_recv[1, piece_rows, :]

            finish(q, depth)

    def settle():
        for q in range(CHUNKS):
            to_right[q].wait_send()
            to_left[q].wait_send()
            onward[q].wait_send()
            across[0][q].wait_send()

            @pl.when(up_there)
            def _():
                across[1][q].wait_send()
                upward[q].wait_send()

            @pl.when(down_there)
            def _():
                across[2][q].wait_send()
                downward[q].wait_send()

    return settle


EXCHANGE_SCRATCH = lambda width: [
    pltpu.VMEM((6, TABLE, 128), f32),
    pltpu.VMEM((3, 2 * width, width), f32),
    pltpu.VMEM((3, 2 * width, width), f32),
    pltpu.VMEM((3, 2 * width, width), f32),
    pltpu.VMEM((2, 2 * width, width), f32),
    pltpu.VMEM((2, 2 * width, width), f32),
    pltpu.VMEM((2 * width, width), f32),
    pltpu.SemaphoreType.DMA((8, CHUNKS)),
    pltpu.SemaphoreType.DMA((8, CHUNKS)),
    pltpu.SemaphoreType.DMA((5,)),
    pltpu.SemaphoreType.DMA((5,)),
]


def born_kernel(
    lines, slabs, width, faces,
    energy_ref, source_ref, index_ref, weights_ref, green_ref, ham_ref, profile_ref, coup_ref, left_ref, right_ref,
    out_ref,
    table_ref, got, part_send, part_recv, line_send, line_recv, acc, piece_send, piece_recv, table_send, table_recv,
    perm_ref, perm_t_ref, next_ref, d_here_ref, d_ref, ends_ref, lead_ref,
    sk_ref, lhs_ref, w_ref, a_ref, b_ref, m_ref, send_ref, send_back_ref, pa_ref, x_ref,
    send_sem, recv_sem,
):
    slab = lax.axis_index("slab")
    F = faces
    row = lax.broadcasted_iota(jnp.int32, (width, width), 0)
    col = lax.broadcasted_iota(jnp.int32, (width, width), 1)
    unit = jnp.where(row == col, 1.0, 0.0)
    barrier, greetings = greet(lines, slabs)
    make_table(source_ref, index_ref, weights_ref, table_ref)
    pl.semaphore_wait(barrier, greetings)
    after, ahead_of = lax.rem(slab + 1, slabs), lax.rem(slab + slabs - 1, slabs)
    forward = remote(send_ref, b_ref, send_sem.at[0], recv_sem.at[0], slab=after)
    backward = remote(send_back_ref, m_ref, send_sem.at[1], recv_sem.at[1], slab=ahead_of)
    give_coupling = remote(coup_ref, next_ref, send_sem.at[2], recv_sem.at[2], slab=ahead_of)
    give_d = remote(d_here_ref, d_ref, send_sem.at[3], recv_sem.at[3], slab=after)
    zero = jnp.zeros((F, F), f32)

    def meanwhile():
        give_coupling.start()
        spot = lax.broadcasted_iota(jnp.int32, (width, F), 0)
        hot_left = jnp.where(spot == left_ref[...], 1.0, 0.0)
        hot_right = jnp.where(spot == right_ref[...], 1.0, 0.0)
        on_face = jnp.sum(hot_left, axis=1, keepdims=True)
        off_face = jnp.broadcast_to(1.0 - on_face, (width, 128)).astype(bf16)
        before = mm(jnp.where(col < row, 1.0, 0.0).astype(bf16), off_face)[:, :1]
        rest = jnp.where(col == F + before.astype(jnp.int32), 1.0 - on_face, 0.0)
        perm_t = rest + lanes(hot_left, jnp.zeros((width, width - F), f32))
        perm_t_ref[...] = perm_t.astype(bf16)
        perm_ref[...] = perm_t.T.astype(bf16)
        order = mm(hot_left.T.astype(bf16), hot_right.astype(bf16)).astype(bf16)
        coup = coup_ref[...]
        lead_ref[...] = -0.5 * mm(left3(coup.T), right3v(coup))
        give_coupling.wait()
        high, low = split(next_ref[...])
        lowest = (next_ref[...] - high.astype(f32) - low.astype(f32)).astype(bf16)
        d_here_ref[...] = mm(lanes(order, order, order), rows(high, low, lowest))
        give_d.start()
        give_d.wait()
        ends_ref[...] = jnp.where(slab < slabs - 1, d_here_ref[...].T, d_ref[...])

    def finish(chunk, depth):
        piece_rows = pl.ds(chunk * depth, depth)
        first = chunk * depth
        imag = first >= width
        there = pl.ds(first - width if imag else first, depth)
        diagonal = jnp.where(
            lax.broadcasted_iota(jnp.int32, (depth, width), 0) + (first - width if imag else first)
            == lax.broadcasted_iota(jnp.int32, (depth, width), 1),
            1.0, 0.0,
        )
        sigma = profile_ref[there, :] * acc[piece_rows, :]
        if imag:
            acc[piece_rows, :] = BROAD * diagonal - sigma
        else:
            acc[piece_rows, :] = energy_ref[...] * diagonal - ham_ref[there, :] - sigma

    settle = exchange(lines, green_ref, table_ref, got, part_send, part_recv, line_send, line_recv, acc,
                      piece_send, piece_recv, table_send, table_recv, meanwhile, finish)

    perm = perm_ref[...]
    pieces = split(acc[:width, :]) + split(acc[width:, :])
    turned = mmt(rows(*pieces), perm).astype(bf16)
    placed = mm(perm, lanes(*[turned[k * width:(k + 1) * width] for k in range(4)]))
    a_real = placed[:, :width] + placed[:, width:2 * width]
    a_imag = placed[:, 2 * width:3 * width] + placed[:, 3 * width:]
    a_ref[:, :width] = a_real
    a_ref[:, width:] = a_imag
    inner = (row < F) & (col < F)
    modulus = jnp.where(inner, 0.0, jnp.sqrt(a_real * a_real + a_imag * a_imag))
    row_sums = jnp.sum(modulus, axis=1, keepdims=True)
    col_sums = jnp.sum(modulus, axis=0, keepdims=True)
    pa_ref[...] = lanes(a_real[:, :F], a_imag[:, :F])
    open_real = jnp.where(inner, 0.0, a_real)
    open_imag = jnp.where(inner, 0.0, a_imag)
    rh, rl = split(open_real)
    ih, il = split(open_imag)
    left = rows(lanes(rh, rh, rl, ih, ih, il), lanes(ih, ih, il, -rh, -rh, -rl))
    sk_ref[...] = mmt(left, lanes(rh, rl, rh, ih, il, ih))

    @pl.when(slab == 0)
    def _():
        b_ref[...] = lanes(jnp.zeros((F, F), f32), lead_ref[...])

    @pl.when(slab > 0)
    def _():
        forward.wait_recv()

    face = pa_ref[:F, :] - b_ref[...]
    pa_ref[:F, :] = face
    square = face * face
    face_mod = jnp.sqrt(square[:, :F] + square[:, F:])
    face_rows = jnp.sum(face_mod, axis=1, keepdims=True) + row_sums[:F]
    face_cols = jnp.sum(face_mod, axis=0, keepdims=True) + col_sums[:, :F]
    row_norm = jnp.maximum(jnp.max(row_sums[F:], axis=0, keepdims=True), jnp.max(face_rows, axis=0, keepdims=True))
    col_norm = jnp.maximum(jnp.max(col_sums[:, F:], axis=1, keepdims=True), jnp.max(face_cols, axis=1, keepdims=True))
    scale = 1.0 / (row_norm * col_norm)
    pa = pa_ref[...]
    other = swapped(face, 1.0, -1.0)
    ends = ends_ref[...]
    first = rows(face, other, lanes(ends, zero), lanes(zero, -ends))
    over = mmt(left3(first), right3(pa))
    down = mmt(left3(pa), right3(rows(face, -other)))
    inside = lax.broadcasted_iota(jnp.int32, (width, 2 * F), 1) < F
    below = (lax.broadcasted_iota(jnp.int32, (width, 2 * F), 0) >= F) & inside
    for part in range(2):
        base = part * width
        sk_ref[base:base + F, :] += over[part * F:(part + 1) * F]
        column = down if part == 0 else lanes(down[:, F:], down[:, :F])
        sk_ref[base:base + width, :2 * F] += jnp.where(below, column, 0.0)
    sym = unit - scale * sk_ref[:width, :]
    skew = -scale * sk_ref[width:, :]
    lr = scale * over[2 * F:3 * F]
    li = scale * over[3 * F:]

    def thin(real, imag):
        return lanes(left3(rows(real, imag)), left3(rows(-imag, real)))

    for level in range(3):
        w_ref[level, :, :] = rows(right3v(sym), right3v(skew))
        lhs_ref[level, :width, :] = lanes(left3(sym + skew), left3(sym - skew))
        lhs_ref[level, width:, :] = thin(lr, li)
        result = mm(lhs_ref[level], w_ref[level])
        grown = result[:width]
        flipped = grown.T
        sym = 0.5 * (grown + flipped)
        skew = 0.5 * (grown - flipped)
        lr = lr + result[width:width + F]
        li = li + result[width + F:]
    w_ref[3, :, :] = rows(right3v(sym), right3v(skew))
    ur, ui = sym[:F], skew[:F]
    result = mm(
        lanes(left3(rows(lr, li, ur, ui)), left3(rows(-li, lr, -ui, ur))), w_ref[3]
    )
    w1r, w1i = ur + unit[:F], ui
    w2r, w2i = ur + result[2 * F:3 * F], ui + result[3 * F:]
    left = left3(lanes(lr, li, result[:F], result[F:2 * F]))
    right = right3(rows(lanes(w1r, w1i, w2r, w2i), lanes(-w1i, w1r, -w2i, w2r)))
    packed = mmt(left, right)
    both = rows(lanes(ends, zero), lanes(zero, ends))
    packed = mmt(left3(packed), right3(both))

    @pl.when(slab < slabs - 1)
    def _():
        send_ref[...] = packed
        forward.start()

    @pl.when(slab == slabs - 1)
    def _():
        send_back_ref[...] = packed
        backward.start()

    lhs_ref[3, :width, :] = lanes(left3(sym + skew), left3(sym - skew))
    first_g = lhs_ref[0, :width, :]
    part_g = first_g[:, :width].astype(f32) + first_g[:, 2 * width:3 * width].astype(f32) + unit
    part_t = first_g[:, 3 * width:4 * width].astype(f32) + first_g[:, 5 * width:].astype(f32) + unit
    for level in range(1, 4):
        part_g = part_g + mm(lanes(left3(part_g), left3(part_t)), w_ref[level])
        part_t = part_g.T
    grown = mm(lhs_ref[3, :width, :], w_ref[3])
    flipped = grown.T
    last = rows(right3v(0.5 * (grown + flipped)), right3v(0.5 * (grown - flipped)))
    part_g = part_g + mm(lanes(left3(part_g), left3(part_t)), last)
    part_t = part_g.T
    pr = 0.5 * (part_g + part_t)
    pi = 0.5 * (part_g - part_t)
    a_ref[:F, :F] = face[:, :F]
    a_ref[:F, width:width + F] = face[:, F:]
    left = lanes(left3(a_ref[:, :width].T), left3(a_ref[:, width:].T))
    right = rows(right3v(lanes(pr, pi)), right3v(lanes(pi, -pr)))
    block = scale * mm(left, right)
    block_face = lanes(block[:F, :F], block[:F, width:width + F])
    hr, qr = split(block[:, :width])
    hi, qi = split(block[:, width:])
    turned = mm(perm_t_ref[...], lanes(hr, qr, hi, qi))
    back = turned.astype(bf16)
    back = mm(rows(*[back[:, k * width:(k + 1) * width] for k in range(4)]), perm)
    x_ref[0] = back[:width] + back[width:2 * width]
    x_ref[1] = back[2 * width:3 * width] + back[3 * width:]

    @pl.when(slab == slabs - 1)
    def _():
        out_ref[0, 0, :, :, :] = x_ref[...]

    @pl.when(slab < slabs - 1)
    def _():
        column = left3(
            lanes(
                turned[:, :F] + turned[:, width:width + F],
                turned[:, 2 * width:2 * width + F] + turned[:, 3 * width:3 * width + F],
            )
        )
        face_rows = mm(rows(hr[:F], qr[:F], hi[:F], qi[:F]), perm)
        rr = face_rows[:F] + face_rows[F:2 * F]
        ri = face_rows[2 * F:3 * F] + face_rows[3 * F:]
        across = right3v(rows(lanes(rr, ri), lanes(-ri, rr)))
        d = d_ref[...]
        d_both = right3(rows(lanes(d, zero), lanes(zero, d)))
        u = left3(mm(left3(d), right3v(block_face)))
        v = right3v(as_right(mmt(left3(block_face), d_both)))
        k = mmt(u, d_both)
        backward.wait_recv()
        incoming = right3v(as_right(m_ref[...]))

        @pl.when(slab > 0)
        def _():
            send_back_ref[...] = k + mm(left3(mm(u, incoming)), v)
            backward.start()

        more = mm(left3(mm(column, incoming)), across)
        out_ref[0, 0, 0, :, :] = x_ref[0] + more[:, :width]
        out_ref[0, 0, 1, :, :] = x_ref[1] + more[:, width:]

    @pl.when(slab < slabs - 1)
    def _():
        forward.wait_send()

    @pl.when(slab > 0)
    def _():
        backward.wait_send()
    settle()


def run(energies, hamiltonian, coupling, green_prev, profile, phonon_weights, source, weight_index, left, right):
    width, faces = hamiltonian.shape[-1], coupling.shape[-1]
    slabs, lines = lax.axis_size("slab"), lax.axis_size("energy") // (NX * CORES)
    vmem, smem = pl.BlockSpec(memory_space=pltpu.VMEM), pl.BlockSpec(memory_space=pltpu.SMEM)
    face_block = pltpu.VMEM((faces, faces), f32)
    face_pair = pltpu.VMEM((faces, 2 * faces), f32)
    return pl.pallas_call(
        functools.partial(born_kernel, lines, slabs, width, faces),
        out_shape=jax.ShapeDtypeStruct((1, 1, 2, width, width), f32),
        in_specs=[vmem, smem, smem, smem] + [vmem] * 6,
        out_specs=vmem,
        scratch_shapes=EXCHANGE_SCRATCH(width) + [
            pltpu.VMEM((width, width), bf16),
            pltpu.VMEM((width, width), bf16),
            face_block, face_block, face_block, face_block, face_block,
            pltpu.VMEM((2 * width, width), f32),
            pltpu.VMEM((4, width + 2 * faces, 6 * width), bf16),
            pltpu.VMEM((4, 6 * width, width), bf16),
            pltpu.VMEM((width, 2 * width), f32),
            face_pair, face_pair, face_pair, face_pair,
            pltpu.VMEM((width, 2 * faces), f32),
            pltpu.VMEM((2, width, width), f32),
            pltpu.SemaphoreType.DMA((4,)),
            pltpu.SemaphoreType.DMA((4,)),
        ],
        compiler_params=pltpu.CompilerParams(
            collective_id=0, has_side_effects=True, vmem_limit_bytes=48 * 1024 * 1024
        ),
        name="born",
    )(
        energies.reshape(1, 1), source, weight_index, phonon_weights,
        green_prev.reshape(2 * width, width), hamiltonian[0], profile, coupling[0], left, right,
    )


def solution(mesh):
    in_specs = (
        P("energy"),
        P("slab", None, None),
        P("slab", None, None),
        P("energy", "slab", None, None, None),
        P(),
        P(),
        P("energy", None),
        P("energy", None),
        P("slab", None),
        P("slab", None),
    )
    out_specs = P("energy", "slab", None, None, None)
    return jax.shard_map(run, mesh=mesh, in_specs=in_specs, out_specs=out_specs, check_vma=False)
```

```python
import functools
import jax
import jax.numpy as jnp
from jax import lax
from jax.experimental import pallas as pl
from jax.experimental.pallas import tpu as pltpu
from jax.sharding import PartitionSpec as P

BROAD = 0.02
f32 = jnp.float32
bf16 = jnp.bfloat16
MESH = pl.DeviceIdType.MESH


def mm(left, right):
    return jnp.dot(left, right, preferred_element_type=f32)


def mmt(left, right):
    return lax.dot_general(left, right, (((1,), (1,)), ((), ())), preferred_element_type=f32)


def split(value):
    high = value.astype(bf16)
    return high, (value - high.astype(f32)).astype(bf16)


def lanes(*pieces):
    return jnp.concatenate(pieces, axis=1)


def rows(*pieces):
    return jnp.concatenate(pieces, axis=0)


def left3(value):
    high, low = split(value)
    return lanes(high, high, low)


def right3(value):
    high, low = split(value)
    return lanes(high, low, high)


def right3v(value):
    high, low = split(value)
    return rows(high, low, high)


def swapped(packed, low_sign, high_sign):
    half = packed.shape[1] // 2
    lane = lax.broadcasted_iota(jnp.int32, packed.shape, 1)
    turned = lanes(packed[:, half:], packed[:, :half])
    return jnp.where(lane < half, low_sign * turned, high_sign * turned)


def put(ref, value):
    high, low = split(value)
    ref[0] = high
    ref[1] = low


def tripled(ref):
    return lanes(ref[0], ref[0], ref[1])


def as_weights(sym_ref, skew_ref):
    return rows(sym_ref[0], sym_ref[1], sym_ref[0], skew_ref[0], skew_ref[1], skew_ref[0])


def across_of(real, imag):
    return right3v(rows(lanes(real, imag), lanes(-imag, real)))


def as_right(packed):
    return rows(packed, swapped(packed, -1.0, 1.0))


NX = 4
CORES = 2
CHUNKS = 8
AHEAD = 3
FAR_LAG = 2
PARTNER_LAG = 3
LINE_LAG = 5
TABLE = 32


def where_on_energy():
    spot = lax.axis_index("energy")
    core = lax.rem(spot, CORES)
    chip = lax.div(spot, CORES)
    return lax.rem(chip, NX), lax.div(chip, NX), core


def energy_of(x, z, core):
    return (z * NX + x) * CORES + core


def remote(source, target, send, recv, **device):
    return pltpu.make_async_remote_copy(
        src_ref=source, dst_ref=target, send_sem=send, recv_sem=recv, device_id=device, device_id_type=MESH
    )


def greet(lines, slabs):
    x, z, core = where_on_energy()
    barrier = pltpu.get_barrier_semaphore()

    def signal(**device):
        pl.semaphore_signal(barrier, inc=1, device_id=device, device_id_type=MESH)

    signal(energy=energy_of(lax.rem(x + 1, NX), z, core))
    signal(energy=energy_of(lax.rem(x + NX - 1, NX), z, core))
    signal(energy=energy_of(x, z, 1 - core))
    count = 3
    for step, there in ((1, z < lines - 1), (-1, z > 0)):
        @pl.when(there)
        def _():
            signal(energy=energy_of(x, z + step, core))
            signal(energy=energy_of(x, z + step, 1 - core))
        count = count + 2 * there.astype(jnp.int32)
    if slabs > 1:
        slab = lax.axis_index("slab")
        for step in range(1, slabs):
            signal(slab=lax.rem(slab + step, slabs))
        count = count + slabs - 1
    return barrier, count


def make_table(source_ref, index_ref, weights_ref, table_ref):
    here = lax.axis_index("energy")
    row = lax.broadcasted_iota(jnp.int32, (TABLE, 128), 0)
    total = jnp.zeros((TABLE, 128), f32)
    for term in range(2):
        weight = weights_ref[index_ref[0, term]]
        distance = source_ref[0, term] - here + TABLE // 2
        total = total + jnp.where(row == distance, weight, 0.0)
    table_ref[0] = total


def exchange(lines, own, table_ref, got, part_send, part_recv, line_send, line_recv, acc,
             send_sem, recv_sem, table_send, table_recv, meanwhile, finish):
    x, z, core = where_on_energy()
    depth = own.shape[0] // CHUNKS
    right = energy_of(lax.rem(x + 1, NX), z, core)
    left = energy_of(lax.rem(x + NX - 1, NX), z, core)
    partner = energy_of(x, z, 1 - core)
    up_there, down_there = z < lines - 1, z > 0
    up, down = energy_of(x, z + 1, core), energy_of(x, z - 1, core)
    up_other, down_other = energy_of(x, z + 1, 1 - core), energy_of(x, z - 1, 1 - core)

    def part(ref, chunk):
        return ref.at[pl.ds(chunk * depth, depth), :]

    def tables(flow, device):
        return remote(table_ref.at[0], table_ref.at[flow + 1], table_send.at[flow], table_recv.at[flow], energy=device)

    to_partner = tables(0, partner)
    to_up, to_up_other = tables(3, up), tables(4, up_other)
    to_down, to_down_other = tables(1, down), tables(2, down_other)

    def piece(flow, chunk, source, target, device):
        return remote(source, target, send_sem.at[flow, chunk], recv_sem.at[flow, chunk], energy=device)

    to_right = [piece(0, q, part(own, q), part(got.at[0], q), right) for q in range(CHUNKS)]
    to_left = [piece(1, q, part(own, q), part(got.at[1], q), left) for q in range(CHUNKS)]
    onward = [
        piece(2, q, part(got.at[q % 2], q), part(got.at[2], q), right if q % 2 == 0 else left)
        for q in range(CHUNKS)
    ]
    across = [
        [piece(3 + k, q, part(part_send.at[k], q), part(part_recv.at[k], q), partner) for q in range(CHUNKS)]
        for k in range(3)
    ]
    upward = [piece(6, q, part(line_send.at[0], q), part(line_recv.at[0], q), up) for q in range(CHUNKS)]
    downward = [piece(7, q, part(line_send.at[1], q), part(line_recv.at[1], q), down) for q in range(CHUNKS)]

    def own_start(chunk):
        to_right[chunk].start()
        to_left[chunk].start()

    for chunk in range(AHEAD):
        own_start(chunk)
    to_partner.start()

    @pl.when(up_there)
    def _():
        to_up.start()
        to_up_other.start()

    @pl.when(down_there)
    def _():
        to_down.start()
        to_down_other.start()

    meanwhile[0]()
    to_partner.wait()

    @pl.when(up_there)
    def _():
        to_up.wait_send()
        to_up_other.wait_send()
        to_down.wait_recv()
        to_down_other.wait_recv()

    @pl.when(down_there)
    def _():
        to_down.wait_send()
        to_down_other.wait_send()
        to_up.wait_recv()
        to_up_other.wait_recv()

    apart = [0] + [lax.rem(x + step, NX) - x for step in (3, 1, 2)]

    def weighted(slot, line, other, chunk):
        total = None
        for k in range(4):
            lag = 2 * apart[k] + (2 * core - 1 if other else 0) - 8 * line + TABLE // 2
            weight = table_ref[slot, pl.ds(lag, 1), :]
            block = (own if k == 0 else got.at[k - 1])[pl.ds(chunk * depth, depth), :]
            term = lanes(weight, weight) * block
            total = term if total is None else total + term
        return total

    for step in range(CHUNKS + LINE_LAG):
        q = step
        if q < CHUNKS:
            to_right[q].wait_recv()
            to_left[q].wait_recv()
            onward[q].start()
            if q + AHEAD < CHUNKS:
                own_start(q + AHEAD)
        if step in (1, 3):
            meanwhile[(step + 1) // 2]()
        q = step - FAR_LAG
        if 0 <= q < CHUNKS:
            onward[q].wait_recv()
            piece_rows = pl.ds(q * depth, depth)
            acc[piece_rows, :] = weighted(0, 0, False, q)
            part_send[0, piece_rows, :] = weighted(1, 0, True, q)
            across[0][q].start()

            @pl.when(up_there)
            def _():
                line_send[0, piece_rows, :] = weighted(2, 1, False, q)
                part_send[1, piece_rows, :] = weighted(3, 1, True, q)
                across[1][q].start()

            @pl.when(down_there)
            def _():
                line_send[1, piece_rows, :] = weighted(4, -1, False, q)
                part_send[2, piece_rows, :] = weighted(5, -1, True, q)
                across[2][q].start()
        q = step - PARTNER_LAG
        if 0 <= q < CHUNKS:
            piece_rows = pl.ds(q * depth, depth)
            across[0][q].wait_recv()
            acc[piece_rows, :] += part_recv[0, piece_rows, :]

            @pl.when(up_there)
            def _():
                across[1][q].wait_recv()
                line_send[0, piece_rows, :] += part_recv[1, piece_rows, :]
                upward[q].start()

            @pl.when(down_there)
            def _():
                across[2][q].wait_recv()
                line_send[1, piece_rows, :] += part_recv[2, piece_rows, :]
                downward[q].start()
        q = step - LINE_LAG
        if 0 <= q < CHUNKS:
            piece_rows = pl.ds(q * depth, depth)

            @pl.when(down_there)
            def _():
                upward[q].wait_recv()
                acc[piece_rows, :] += line_recv[0, piece_rows, :]

            @pl.when(up_there)
            def _():
                downward[q].wait_recv()
                acc[piece_rows, :] += line_recv[1, piece_rows, :]

            finish(q, depth)

    def settle():
        for q in range(CHUNKS):
            to_right[q].wait_send()
            to_left[q].wait_send()
            onward[q].wait_send()
            across[0][q].wait_send()

            @pl.when(up_there)
            def _():
                across[1][q].wait_send()
                upward[q].wait_send()

            @pl.when(down_there)
            def _():
                across[2][q].wait_send()
                downward[q].wait_send()

    return settle


EXCHANGE_SCRATCH = lambda width: [
    pltpu.VMEM((6, TABLE, 128), f32),
    pltpu.VMEM((3, 2 * width, width), f32),
    pltpu.VMEM((3, 2 * width, width), f32),
    pltpu.VMEM((3, 2 * width, width), f32),
    pltpu.VMEM((2, 2 * width, width), f32),
    pltpu.VMEM((2, 2 * width, width), f32),
    pltpu.VMEM((2 * width, width), f32),
    pltpu.SemaphoreType.DMA((8, CHUNKS)),
    pltpu.SemaphoreType.DMA((8, CHUNKS)),
    pltpu.SemaphoreType.DMA((5,)),
    pltpu.SemaphoreType.DMA((5,)),
]


def born_kernel(
    lines, slabs, width, faces,
    energy_ref, source_ref, index_ref, weights_ref, green_ref, ham_ref, profile_ref, coup_ref, left_ref, right_ref,
    out_ref,
    table_ref, got, part_send, part_recv, line_send, line_recv, acc, piece_send, piece_recv, table_send, table_recv,
    perm_ref, perm_t_ref, next_ref, order_ref, d_all, face_all, ends_ref, lead_ref,
    sk_ref, g_ref, t_ref, s_ref, k_ref, thin_ref, a_ref, b_ref, m_ref, send_ref, part_ref, pa_ref, x_ref,
    send_sem, recv_sem, spread_sem, d_sem, face_sem,
):
    slab = lax.axis_index("slab")
    F = faces
    row = lax.broadcasted_iota(jnp.int32, (width, width), 0)
    col = lax.broadcasted_iota(jnp.int32, (width, width), 1)
    unit = jnp.where(row == col, 1.0, 0.0)
    barrier, greetings = greet(lines, slabs)
    make_table(source_ref, index_ref, weights_ref, table_ref)
    pl.semaphore_wait(barrier, greetings)
    last = slabs - 1
    forward = remote(send_ref, b_ref, send_sem.at[0], recv_sem.at[0], slab=lax.rem(slab + 1, slabs))
    give_coupling = remote(coup_ref, next_ref, send_sem.at[1], recv_sem.at[1], slab=lax.rem(slab + last, slabs))
    messages = [remote(send_ref, m_ref, spread_sem.at[0, t], recv_sem.at[2], slab=t) for t in range(last)]
    give_d = [
        remote(d_all.at[slab], d_all.at[slab], spread_sem.at[1, t], d_sem.at[slab], slab=t) for t in range(slabs)
    ]
    give_face = [
        remote(face_all.at[slab], face_all.at[slab], spread_sem.at[2, t], face_sem.at[slab], slab=t)
        for t in range(last)
    ]

    def d_goes(t):
        return (slab == last - 1) if t == last else ((slab > t) & (slab < last - 1))

    def face_goes(t):
        return (slab > t) & (slab < last)

    zero = jnp.zeros((F, F), f32)

    def first_stage():
        give_coupling.start()
        spot = lax.broadcasted_iota(jnp.int32, (width, F), 0)
        hot_left = jnp.where(spot == left_ref[...], 1.0, 0.0)
        hot_right = jnp.where(spot == right_ref[...], 1.0, 0.0)
        on_face = jnp.sum(hot_left, axis=1, keepdims=True)
        off_face = jnp.broadcast_to(1.0 - on_face, (width, 128)).astype(bf16)
        before = mm(jnp.where(col < row, 1.0, 0.0).astype(bf16), off_face)[:, :1]
        rest = jnp.where(col == F + before.astype(jnp.int32), 1.0 - on_face, 0.0)
        perm_t = rest + lanes(hot_left, jnp.zeros((width, width - F), f32))
        perm_t_ref[...] = perm_t.astype(bf16)
        perm_ref[...] = perm_t.T.astype(bf16)
        order_ref[...] = mm(hot_left.T.astype(bf16), hot_right.astype(bf16)).astype(bf16)
        coup = coup_ref[...]
        lead_ref[...] = -0.5 * mm(left3(coup.T), right3v(coup))

    def second_stage():
        give_coupling.wait()
        following = next_ref[...]
        high, low = split(following)
        lowest = (following - high.astype(f32) - low.astype(f32)).astype(bf16)
        order = order_ref[...]
        here = mm(lanes(order, order, order), rows(high, low, lowest))
        d_all[slab] = here
        ends_ref[...] = here.T
        for t in range(slabs):
            @pl.when(d_goes(t))
            def _():
                give_d[t].start()

    def third_stage():
        def arrived(t, carry):
            remote(d_all.at[t], d_all.at[t], spread_sem.at[1, 0], d_sem.at[t], slab=slab).wait_recv()
            return carry

        lax.fori_loop(slab + 1, last - 1, arrived, 0)

        @pl.when(slab == last)
        def _():
            arrived(last - 1, 0)
            ends_ref[...] = d_all[last - 1]

    def finish(chunk, depth):
        piece_rows = pl.ds(chunk * depth, depth)
        first = chunk * depth
        imag = first >= width
        there = pl.ds(first - width if imag else first, depth)
        diagonal = jnp.where(
            lax.broadcasted_iota(jnp.int32, (depth, width), 0) + (first - width if imag else first)
            == lax.broadcasted_iota(jnp.int32, (depth, width), 1),
            1.0, 0.0,
        )
        sigma = profile_ref[there, :] * acc[piece_rows, :]
        if imag:
            acc[piece_rows, :] = BROAD * diagonal - sigma
        else:
            acc[piece_rows, :] = energy_ref[...] * diagonal - ham_ref[there, :] - sigma

    settle = exchange(lines, green_ref, table_ref, got, part_send, part_recv, line_send, line_recv, acc,
                      piece_send, piece_recv, table_send, table_recv,
                      (first_stage, second_stage, third_stage), finish)

    perm = perm_ref[...]
    pieces = split(acc[:width, :]) + split(acc[width:, :])
    turned = mmt(rows(*pieces), perm).astype(bf16)
    placed = mm(perm, lanes(*[turned[k * width:(k + 1) * width] for k in range(4)]))
    a_real = placed[:, :width] + placed[:, width:2 * width]
    a_imag = placed[:, 2 * width:3 * width] + placed[:, 3 * width:]
    a_ref[:, :width] = a_real
    a_ref[:, width:] = a_imag
    inner = (row < F) & (col < F)
    modulus = jnp.where(inner, 0.0, jnp.sqrt(a_real * a_real + a_imag * a_imag))
    row_sums = jnp.sum(modulus, axis=1, keepdims=True)
    col_sums = jnp.sum(modulus, axis=0, keepdims=True)
    pa_ref[...] = lanes(a_real[:, :F], a_imag[:, :F])
    open_real = jnp.where(inner, 0.0, a_real)
    open_imag = jnp.where(inner, 0.0, a_imag)
    rh, rl = split(open_real)
    ih, il = split(open_imag)
    left = rows(lanes(rh, rh, rl, ih, ih, il), lanes(ih, ih, il, -rh, -rh, -rl))
    sk_ref[...] = mmt(left, lanes(rh, rl, rh, ih, il, ih))

    @pl.when(slab == 0)
    def _():
        b_ref[...] = lanes(jnp.zeros((F, F), f32), lead_ref[...])

    @pl.when(slab > 0)
    def _():
        forward.wait_recv()

    face = pa_ref[:F, :] - b_ref[...]
    pa_ref[:F, :] = face
    square = face * face
    face_mod = jnp.sqrt(square[:, :F] + square[:, F:])
    face_rows = jnp.sum(face_mod, axis=1, keepdims=True) + row_sums[:F]
    face_cols = jnp.sum(face_mod, axis=0, keepdims=True) + col_sums[:, :F]
    row_norm = jnp.maximum(jnp.max(row_sums[F:], axis=0, keepdims=True), jnp.max(face_rows, axis=0, keepdims=True))
    col_norm = jnp.maximum(jnp.max(col_sums[:, F:], axis=1, keepdims=True), jnp.max(face_cols, axis=1, keepdims=True))
    scale = 1.0 / (row_norm * col_norm)
    pa = pa_ref[...]
    other = swapped(face, 1.0, -1.0)
    ends = ends_ref[...]
    first = rows(face, other, lanes(ends, zero), lanes(zero, -ends))
    over = mmt(left3(first), right3(pa))
    down = mmt(left3(pa), right3(rows(face, -other)))
    inside = lax.broadcasted_iota(jnp.int32, (width, 2 * F), 1) < F
    below = (lax.broadcasted_iota(jnp.int32, (width, 2 * F), 0) >= F) & inside
    for part in range(2):
        base = part * width
        sk_ref[base:base + F, :] += over[part * F:(part + 1) * F]
        column = down if part == 0 else lanes(down[:, F:], down[:, :F])
        sk_ref[base:base + width, :2 * F] += jnp.where(below, column, 0.0)
    sym = unit - scale * sk_ref[:width, :]
    skew = -scale * sk_ref[width:, :]
    lr = scale * over[2 * F:3 * F]
    li = scale * over[3 * F:]

    for level in range(3):
        put(s_ref.at[level], sym)
        put(k_ref.at[level], skew)
        put(g_ref.at[level], sym + skew)
        put(t_ref.at[level], sym - skew)
        put(thin_ref.at[0], rows(lr, li))
        put(thin_ref.at[1], rows(-li, lr))
        weights = as_weights(s_ref.at[level], k_ref.at[level])
        grown = mm(lanes(tripled(g_ref.at[level]), tripled(t_ref.at[level])), weights)
        flipped = grown.T
        sym = 0.5 * (grown + flipped)
        skew = 0.5 * (grown - flipped)
        result = mm(lanes(tripled(thin_ref.at[0]), tripled(thin_ref.at[1])), weights)
        lr = lr + result[:F]
        li = li + result[F:]
    put(s_ref.at[3], sym)
    put(k_ref.at[3], skew)
    ur, ui = sym[:F], skew[:F]
    result = mm(
        lanes(left3(rows(lr, li, ur, ui)), left3(rows(-li, lr, -ui, ur))), as_weights(s_ref.at[3], k_ref.at[3])
    )
    w1r, w1i = ur + unit[:F], ui
    w2r, w2i = ur + result[2 * F:3 * F], ui + result[3 * F:]
    left = left3(lanes(lr, li, result[:F], result[F:2 * F]))
    right = right3(rows(lanes(w1r, w1i, w2r, w2i), lanes(-w1i, w1r, -w2i, w2r)))
    packed = mmt(left, right)
    both = rows(lanes(ends, zero), lanes(zero, ends))
    packed = mmt(left3(packed), right3(both))

    send_ref[...] = packed

    @pl.when(slab < last)
    def _():
        forward.start()

    @pl.when(slab == last)
    def _():
        for t in (3, 2, 4, 1, 5, 0, 6):
            messages[t].start()

    put(g_ref.at[3], sym + skew)
    put(t_ref.at[3], sym - skew)
    part_g = g_ref[0, 0].astype(f32) + g_ref[0, 1].astype(f32) + unit
    part_t = t_ref[0, 0].astype(f32) + t_ref[0, 1].astype(f32) + unit
    for level in range(1, 4):
        part_g = part_g + mm(lanes(left3(part_g), left3(part_t)), as_weights(s_ref.at[level], k_ref.at[level]))
        part_t = part_g.T
    grown = mm(lanes(tripled(g_ref.at[3]), tripled(t_ref.at[3])), as_weights(s_ref.at[3], k_ref.at[3]))
    flipped = grown.T
    highest = rows(right3v(0.5 * (grown + flipped)), right3v(0.5 * (grown - flipped)))
    part_g = part_g + mm(lanes(left3(part_g), left3(part_t)), highest)
    part_t = part_g.T
    pr = 0.5 * (part_g + part_t)
    pi = 0.5 * (part_g - part_t)
    a_ref[:F, :F] = face[:, :F]
    a_ref[:F, width:width + F] = face[:, F:]
    left = lanes(left3(a_ref[:, :width].T), left3(a_ref[:, width:].T))
    right = rows(right3v(lanes(pr, pi)), right3v(lanes(pi, -pr)))
    block = scale * mm(left, right)
    block_face = lanes(block[:F, :F], block[:F, width:width + F])
    face_all[slab] = block_face
    for t in (2, 1, 3, 0, 4, 5):
        @pl.when(face_goes(t))
        def _():
            give_face[t].start()

    hr, qr = split(block[:, :width])
    hi, qi = split(block[:, width:])
    turned = mm(perm_t_ref[...], lanes(hr, qr, hi, qi))
    back = turned.astype(bf16)
    back = mm(rows(*[back[:, k * width:(k + 1) * width] for k in range(4)]), perm)
    x_ref[0] = back[:width] + back[width:2 * width]
    x_ref[1] = back[2 * width:3 * width] + back[3 * width:]

    @pl.when(slab == last)
    def _():
        out_ref[0, 0, :, :, :] = x_ref[...]

    @pl.when(slab < last)
    def _():
        column = left3(
            lanes(
                turned[:, :F] + turned[:, width:width + F],
                turned[:, 2 * width:2 * width + F] + turned[:, 3 * width:3 * width + F],
            )
        )
        face_rows = mm(rows(hr[:F], qr[:F], hi[:F], qi[:F]), perm)
        rr = face_rows[:F] + face_rows[F:2 * F]
        ri = face_rows[2 * F:3 * F] + face_rows[3 * F:]
        across = across_of(rr, ri)
        one = unit[:F, :2 * F]
        part_ref[0] = jnp.zeros((F, 2 * F), f32)
        part_ref[1] = one
        part_ref[2] = one

        def compose(t, carry):
            remote(face_all.at[t], face_all.at[t], spread_sem.at[2, 0], face_sem.at[t], slab=slab).wait_recv()
            g = face_all[t]
            d = d_all[t - 1]
            both = right3(rows(lanes(d, zero), lanes(zero, d)))
            u = mm(left3(d), right3v(g))
            v = mmt(left3(g), both)
            k = mmt(left3(u), both)
            before, behind = part_ref[1], right3v(as_right(part_ref[2]))
            before = left3(before)
            part_ref[0] += mm(left3(mm(before, right3v(as_right(k)))), behind)
            part_ref[1] = mm(before, right3v(as_right(u)))
            part_ref[2] = mm(left3(v), behind)
            return carry

        lax.fori_loop(slab + 1, last, compose, 0)
        wide = mm(column, lanes(right3v(as_right(part_ref[0])), right3v(as_right(part_ref[1]))))
        more = mm(left3(wide[:, :2 * F]), across)
        x_ref[0] += more[:, :width]
        x_ref[1] += more[:, width:]
        column = left3(wide[:, 2 * F:])
        across = mm(left3(part_ref[2]), across_of(rr, ri))
        rr, ri = across[:, :width], across[:, width:]
        across = across_of(rr, ri)
        messages[0].wait_recv()
        incoming = right3v(as_right(m_ref[...]))
        more = mm(left3(mm(column, incoming)), across)
        out_ref[0, 0, 0, :, :] = x_ref[0] + more[:, :width]
        out_ref[0, 0, 1, :, :] = x_ref[1] + more[:, width:]

    @pl.when(slab < last)
    def _():
        forward.wait_send()

    @pl.when(slab == last)
    def _():
        for t in range(last):
            messages[t].wait_send()

    for t in range(slabs):
        @pl.when(d_goes(t))
        def _():
            give_d[t].wait_send()

        if t < last:
            @pl.when(face_goes(t))
            def _():
                give_face[t].wait_send()

    settle()


def run(energies, hamiltonian, coupling, green_prev, profile, phonon_weights, source, weight_index, left, right):
    width, faces = hamiltonian.shape[-1], coupling.shape[-1]
    slabs, lines = lax.axis_size("slab"), lax.axis_size("energy") // (NX * CORES)
    vmem, smem = pl.BlockSpec(memory_space=pltpu.VMEM), pl.BlockSpec(memory_space=pltpu.SMEM)
    face_block = pltpu.VMEM((faces, faces), f32)
    face_pair = pltpu.VMEM((faces, 2 * faces), f32)
    return pl.pallas_call(
        functools.partial(born_kernel, lines, slabs, width, faces),
        out_shape=jax.ShapeDtypeStruct((1, 1, 2, width, width), f32),
        in_specs=[vmem, smem, smem, smem] + [vmem] * 6,
        out_specs=vmem,
        scratch_shapes=EXCHANGE_SCRATCH(width) + [
            pltpu.VMEM((width, width), bf16),
            pltpu.VMEM((width, width), bf16),
            face_block,
            pltpu.VMEM((faces, faces), bf16),
            pltpu.VMEM((slabs, faces, faces), f32),
            pltpu.VMEM((slabs, faces, 2 * faces), f32),
            face_block, face_block,
            pltpu.VMEM((2 * width, width), f32),
            pltpu.VMEM((4, 2, width, width), bf16),
            pltpu.VMEM((4, 2, width, width), bf16),
            pltpu.VMEM((4, 2, width, width), bf16),
            pltpu.VMEM((4, 2, width, width), bf16),
            pltpu.VMEM((2, 2, 2 * faces, width), bf16),
            pltpu.VMEM((width, 2 * width), f32),
            face_pair, face_pair, face_pair,
            pltpu.VMEM((3, faces, 2 * faces), f32),
            pltpu.VMEM((width, 2 * faces), f32),
            pltpu.VMEM((2, width, width), f32),
            pltpu.SemaphoreType.DMA((2,)),
            pltpu.SemaphoreType.DMA((3,)),
            pltpu.SemaphoreType.DMA((3, slabs)),
            pltpu.SemaphoreType.DMA((slabs,)),
            pltpu.SemaphoreType.DMA((slabs,)),
        ],
        compiler_params=pltpu.CompilerParams(
            collective_id=0, has_side_effects=True, vmem_limit_bytes=48 * 1024 * 1024
        ),
        name="born",
    )(
        energies.reshape(1, 1), source, weight_index, phonon_weights,
        green_prev.reshape(2 * width, width), hamiltonian[0], profile, coupling[0], left, right,
    )


def solution(mesh):
    in_specs = (
        P("energy"),
        P("slab", None, None),
        P("slab", None, None),
        P("energy", "slab", None, None, None),
        P(),
        P(),
        P("energy", None),
        P("energy", None),
        P("slab", None),
        P("slab", None),
    )
    out_specs = P("energy", "slab", None, None, None)
    return jax.shard_map(run, mesh=mesh, in_specs=in_specs, out_specs=out_specs, check_vma=False)
```

```python
import functools
import jax
import jax.numpy as jnp
from jax import lax
from jax.experimental import pallas as pl
from jax.experimental.pallas import tpu as pltpu
from jax.sharding import PartitionSpec as P

BROAD = 0.02
f32 = jnp.float32
bf16 = jnp.bfloat16
MESH = pl.DeviceIdType.MESH


def mm(left, right):
    return jnp.dot(left, right, preferred_element_type=f32)


def mmt(left, right):
    return lax.dot_general(left, right, (((1,), (1,)), ((), ())), preferred_element_type=f32)


def split(value):
    high = value.astype(bf16)
    return high, (value - high.astype(f32)).astype(bf16)


def lanes(*pieces):
    return jnp.concatenate(pieces, axis=1)


def rows(*pieces):
    return jnp.concatenate(pieces, axis=0)


def left3(value):
    high, low = split(value)
    return lanes(high, high, low)


def right3(value):
    high, low = split(value)
    return lanes(high, low, high)


def right3v(value):
    high, low = split(value)
    return rows(high, low, high)


def swapped(packed, low_sign, high_sign):
    half = packed.shape[1] // 2
    lane = lax.broadcasted_iota(jnp.int32, packed.shape, 1)
    turned = lanes(packed[:, half:], packed[:, :half])
    return jnp.where(lane < half, low_sign * turned, high_sign * turned)


def put(ref, value):
    high, low = split(value)
    ref[0] = high
    ref[1] = low


def tripled(ref):
    return lanes(ref[0], ref[0], ref[1])


def as_weights(sym_ref, skew_ref):
    return rows(sym_ref[0], sym_ref[1], sym_ref[0], skew_ref[0], skew_ref[1], skew_ref[0])


def across_of(real, imag):
    return right3v(rows(lanes(real, imag), lanes(-imag, real)))


def as_right(packed):
    return rows(packed, swapped(packed, -1.0, 1.0))


NX = 4
CORES = 2
DEPTHS = (64,) * 8
CHUNKS = len(DEPTHS)
AHEAD = 3
FAR_LAG = 2
PARTNER_LAG = 3
LINE_LAG = 5
MEANWHILE = (1, 2, 3, 6)
TABLE = 32


def where_on_energy():
    spot = lax.axis_index("energy")
    core = lax.rem(spot, CORES)
    chip = lax.div(spot, CORES)
    return lax.rem(chip, NX), lax.div(chip, NX), core


def energy_of(x, z, core):
    return (z * NX + x) * CORES + core


def remote(source, target, send, recv, **device):
    return pltpu.make_async_remote_copy(
        src_ref=source, dst_ref=target, send_sem=send, recv_sem=recv, device_id=device, device_id_type=MESH
    )


def greet(lines, slabs):
    x, z, core = where_on_energy()
    barrier = pltpu.get_barrier_semaphore()

    def signal(**device):
        pl.semaphore_signal(barrier, inc=1, device_id=device, device_id_type=MESH)

    signal(energy=energy_of(lax.rem(x + 1, NX), z, core))
    signal(energy=energy_of(lax.rem(x + NX - 1, NX), z, core))
    signal(energy=energy_of(x, z, 1 - core))
    count = 3
    for step, there in ((1, z < lines - 1), (-1, z > 0)):
        @pl.when(there)
        def _():
            signal(energy=energy_of(x, z + step, core))
            signal(energy=energy_of(x, z + step, 1 - core))
        count = count + 2 * there.astype(jnp.int32)
    if slabs > 1:
        slab = lax.axis_index("slab")
        for step in (1, slabs - 1):
            signal(slab=lax.rem(slab + step, slabs))
        count = count + 2
    return barrier, count


def make_table(source_ref, index_ref, weights_ref, table_ref):
    here = lax.axis_index("energy")
    row = lax.broadcasted_iota(jnp.int32, (TABLE, 128), 0)
    total = jnp.zeros((TABLE, 128), f32)
    for term in range(2):
        weight = weights_ref[index_ref[0, term]]
        distance = source_ref[0, term] - here + TABLE // 2
        total = total + jnp.where(row == distance, weight, 0.0)
    table_ref[0] = total


def exchange(lines, green, own, table_ref, got, part_send, part_recv, line_send, line_recv, acc,
             send_sem, recv_sem, table_send, table_recv, meanwhile, finish):
    x, z, core = where_on_energy()
    starts = [sum(DEPTHS[:q]) for q in range(CHUNKS)]
    right = energy_of(lax.rem(x + 1, NX), z, core)
    left = energy_of(lax.rem(x + NX - 1, NX), z, core)
    partner = energy_of(x, z, 1 - core)
    up_there, down_there = z < lines - 1, z > 0
    up, down = energy_of(x, z + 1, core), energy_of(x, z - 1, core)
    up_other, down_other = energy_of(x, z + 1, 1 - core), energy_of(x, z - 1, 1 - core)

    def span(chunk):
        return pl.ds(starts[chunk], DEPTHS[chunk])

    def part(ref, chunk):
        return ref.at[span(chunk), :]

    def tables(flow, device):
        return remote(table_ref.at[0], table_ref.at[flow + 1], table_send.at[flow], table_recv.at[flow], energy=device)

    to_partner = tables(0, partner)
    to_up, to_up_other = tables(3, up), tables(4, up_other)
    to_down, to_down_other = tables(1, down), tables(2, down_other)

    def piece(flow, chunk, source, target, device):
        return remote(source, target, send_sem.at[flow, chunk], recv_sem.at[flow, chunk], energy=device)

    to_right = [piece(0, q, part(green, q), part(got.at[0], q), right) for q in range(CHUNKS)]
    to_left = [piece(1, q, part(green, q), part(got.at[1], q), left) for q in range(CHUNKS)]
    onward = [
        piece(2, q, part(got.at[q % 2], q), part(got.at[2], q), right if q % 2 == 0 else left)
        for q in range(CHUNKS)
    ]
    across = [
        [piece(3 + k, q, part(part_send.at[k], q), part(part_recv.at[k], q), partner) for q in range(CHUNKS)]
        for k in range(3)
    ]
    upward = [piece(6, q, part(line_send.at[0], q), part(line_recv.at[0], q), up) for q in range(CHUNKS)]
    downward = [piece(7, q, part(line_send.at[1], q), part(line_recv.at[1], q), down) for q in range(CHUNKS)]

    def own_start(chunk):
        to_right[chunk].start()
        to_left[chunk].start()

    for chunk in range(AHEAD):
        own_start(chunk)
    to_partner.start()

    @pl.when(up_there)
    def _():
        to_up.start()
        to_up_other.start()

    @pl.when(down_there)
    def _():
        to_down.start()
        to_down_other.start()

    meanwhile[0]()
    to_partner.wait()

    @pl.when(up_there)
    def _():
        to_up.wait_send()
        to_up_other.wait_send()
        to_down.wait_recv()
        to_down_other.wait_recv()

    @pl.when(down_there)
    def _():
        to_down.wait_send()
        to_down_other.wait_send()
        to_up.wait_recv()
        to_up_other.wait_recv()

    apart = [0] + [lax.rem(x + step, NX) - x for step in (3, 1, 2)]

    def weighted(slot, line, other, chunk):
        total = None
        for k in range(4):
            lag = 2 * apart[k] + (2 * core - 1 if other else 0) - 8 * line + TABLE // 2
            weight = table_ref[slot, pl.ds(lag, 1), :]
            block = (own if k == 0 else got.at[k - 1])[span(chunk), :]
            term = lanes(weight, weight) * block
            total = term if total is None else total + term
        return total

    for step in range(CHUNKS + LINE_LAG):
        q = step
        if q < CHUNKS:
            to_right[q].wait_recv()
            to_left[q].wait_recv()
            onward[q].start()
            if q + AHEAD < CHUNKS:
                own_start(q + AHEAD)
        if step in MEANWHILE:
            meanwhile[1 + MEANWHILE.index(step)]()
        q = step - FAR_LAG
        if 0 <= q < CHUNKS:
            onward[q].wait_recv()
            piece_rows = span(q)
            acc[piece_rows, :] = weighted(0, 0, False, q)
            part_send[0, piece_rows, :] = weighted(1, 0, True, q)
            across[0][q].start()

            @pl.when(up_there)
            def _():
                line_send[0, piece_rows, :] = weighted(2, 1, False, q)
                part_send[1, piece_rows, :] = weighted(3, 1, True, q)
                across[1][q].start()

            @pl.when(down_there)
            def _():
                line_send[1, piece_rows, :] = weighted(4, -1, False, q)
                part_send[2, piece_rows, :] = weighted(5, -1, True, q)
                across[2][q].start()
        q = step - PARTNER_LAG
        if 0 <= q < CHUNKS:
            piece_rows = span(q)
            across[0][q].wait_recv()
            acc[piece_rows, :] += part_recv[0, piece_rows, :]

            @pl.when(up_there)
            def _():
                across[1][q].wait_recv()
                line_send[0, piece_rows, :] += part_recv[1, piece_rows, :]
                upward[q].start()

            @pl.when(down_there)
            def _():
                across[2][q].wait_recv()
                line_send[1, piece_rows, :] += part_recv[2, piece_rows, :]
                downward[q].start()
        q = step - LINE_LAG
        if 0 <= q < CHUNKS:
            piece_rows = span(q)

            @pl.when(down_there)
            def _():
                upward[q].wait_recv()
                acc[piece_rows, :] += line_recv[0, piece_rows, :]

            @pl.when(up_there)
            def _():
                downward[q].wait_recv()
                acc[piece_rows, :] += line_recv[1, piece_rows, :]

            finish(starts[q], DEPTHS[q])

    def settle():
        for q in range(CHUNKS):
            to_right[q].wait_send()
            to_left[q].wait_send()
            onward[q].wait_send()
            across[0][q].wait_send()

            @pl.when(up_there)
            def _():
                across[1][q].wait_send()
                upward[q].wait_send()

            @pl.when(down_there)
            def _():
                across[2][q].wait_send()
                downward[q].wait_send()

    return settle


EXCHANGE_SCRATCH = lambda width: [
    pltpu.VMEM((6, TABLE, 128), f32),
    pltpu.VMEM((3, 2 * width, width), f32),
    pltpu.VMEM((3, 2 * width, width), f32),
    pltpu.VMEM((3, 2 * width, width), f32),
    pltpu.VMEM((2, 2 * width, width), f32),
    pltpu.VMEM((2, 2 * width, width), f32),
    pltpu.VMEM((2 * width, width), f32),
    pltpu.SemaphoreType.DMA((8, CHUNKS)),
    pltpu.SemaphoreType.DMA((8, CHUNKS)),
    pltpu.SemaphoreType.DMA((5,)),
    pltpu.SemaphoreType.DMA((5,)),
]


def born_kernel(
    lines, slabs, width, faces,
    energy_ref, source_ref, index_ref, weights_ref, green_in, ham_in, profile_in, coup_in, left_in, right_in,
    out_ref,
    green_ref, ham_ref, profile_ref, coup_ref, left_ref, right_ref, load_sem,
    table_ref, got, part_send, part_recv, line_send, line_recv, acc, piece_send, piece_recv, table_send, table_recv,
    perm_ref, perm_t_ref, next_ref, order_ref, d_all, face_all, ends_ref, lead_ref,
    sk_ref, g_ref, t_ref, s_ref, k_ref, thin_ref, a_ref, b_ref, m_ref, send_ref, part_ref, pa_ref, x_ref,
    send_sem, recv_sem, spread_sem, d_sem, face_sem, known_sem,
):
    slab = lax.axis_index("slab")
    F = faces
    row = lax.broadcasted_iota(jnp.int32, (width, width), 0)
    col = lax.broadcasted_iota(jnp.int32, (width, width), 1)
    unit = jnp.where(row == col, 1.0, 0.0)
    barrier, greetings = greet(lines, slabs)
    loads = [
        pltpu.make_async_copy(source, target, load_sem.at[k])
        for k, (source, target) in enumerate((
            (coup_in, coup_ref), (left_in, left_ref), (right_in, right_ref),
            (green_in, green_ref), (ham_in, ham_ref), (profile_in, profile_ref),
        ))
    ]
    for load in loads:
        load.start()
    make_table(source_ref, index_ref, weights_ref, table_ref)
    pl.semaphore_wait(barrier, greetings)
    last = slabs - 1
    forward = remote(send_ref, b_ref, send_sem.at[0], recv_sem.at[0], slab=lax.rem(slab + 1, slabs))
    give_coupling = remote(coup_ref, next_ref, send_sem.at[1], recv_sem.at[1], slab=lax.rem(slab + last, slabs))
    messages = [remote(send_ref, m_ref, spread_sem.at[0, t], recv_sem.at[2], slab=t) for t in range(last)]
    give_d = [
        remote(d_all.at[slab], d_all.at[slab], spread_sem.at[1, t], d_sem.at[slab], slab=t) for t in range(slabs)
    ]
    give_face = [
        remote(face_all.at[slab], face_all.at[slab], spread_sem.at[2, t], face_sem.at[slab], slab=t)
        for t in range(last)
    ]

    def d_goes(t):
        return (slab == last - 1) if t == last else ((slab > t) & (slab < last - 1))

    def face_goes(t):
        return (slab > t) & (slab < last)

    zero = jnp.zeros((F, F), f32)

    def tell(hop):
        for step in (1, last):
            pl.semaphore_signal(
                known_sem.at[hop], inc=1, device_id={"slab": lax.rem(slab + step, slabs)}, device_id_type=MESH
            )

    def first_stage():
        tell(0)
        for load in loads:
            load.wait()
        give_coupling.start()
        spot = lax.broadcasted_iota(jnp.int32, (width, F), 0)
        hot_left = jnp.where(spot == left_ref[...], 1.0, 0.0)
        hot_right = jnp.where(spot == right_ref[...], 1.0, 0.0)
        on_face = jnp.sum(hot_left, axis=1, keepdims=True)
        off_face = jnp.broadcast_to(1.0 - on_face, (width, 128)).astype(bf16)
        before = mm(jnp.where(col < row, 1.0, 0.0).astype(bf16), off_face)[:, :1]
        rest = jnp.where(col == F + before.astype(jnp.int32), 1.0 - on_face, 0.0)
        perm_t = rest + lanes(hot_left, jnp.zeros((width, width - F), f32))
        perm_t_ref[...] = perm_t.astype(bf16)
        perm_ref[...] = perm_t.T.astype(bf16)
        order_ref[...] = mm(hot_left.T.astype(bf16), hot_right.astype(bf16)).astype(bf16)
        coup = coup_ref[...]
        lead_ref[...] = -0.5 * mm(left3(coup.T), right3v(coup))

    def hear_stage():
        pl.semaphore_wait(known_sem.at[0], 2)
        tell(1)

    def second_stage():
        pl.semaphore_wait(known_sem.at[1], 2)
        tell(2)
        give_coupling.wait()
        following = next_ref[...]
        high, low = split(following)
        lowest = (following - high.astype(f32) - low.astype(f32)).astype(bf16)
        order = order_ref[...]
        here = mm(lanes(order, order, order), rows(high, low, lowest))
        d_all[slab] = here
        ends_ref[...] = here.T

    def spread_stage():
        pl.semaphore_wait(known_sem.at[2], 2)
        for t in range(slabs):
            @pl.when(d_goes(t))
            def _():
                give_d[t].start()

    def third_stage():
        def arrived(t, carry):
            remote(d_all.at[t], d_all.at[t], spread_sem.at[1, 0], d_sem.at[t], slab=slab).wait_recv()
            return carry

        lax.fori_loop(slab + 1, last - 1, arrived, 0)

        @pl.when(slab == last)
        def _():
            arrived(last - 1, 0)
            ends_ref[...] = d_all[last - 1]

    def finish(first, depth):
        piece_rows = pl.ds(first, depth)
        imag = first >= width
        there = pl.ds(first - width if imag else first, depth)
        diagonal = jnp.where(
            lax.broadcasted_iota(jnp.int32, (depth, width), 0) + (first - width if imag else first)
            == lax.broadcasted_iota(jnp.int32, (depth, width), 1),
            1.0, 0.0,
        )
        sigma = profile_ref[there, :] * acc[piece_rows, :]
        if imag:
            acc[piece_rows, :] = BROAD * diagonal - sigma
        else:
            acc[piece_rows, :] = energy_ref[0] * diagonal - ham_ref[there, :] - sigma

    settle = exchange(lines, green_in, green_ref, table_ref, got, part_send, part_recv, line_send, line_recv, acc,
                      piece_send, piece_recv, table_send, table_recv,
                      (first_stage, hear_stage, second_stage, spread_stage, third_stage), finish)

    perm = perm_ref[...]
    pieces = split(acc[:width, :]) + split(acc[width:, :])
    turned = mmt(rows(*pieces), perm).astype(bf16)
    placed = mm(perm, lanes(*[turned[k * width:(k + 1) * width] for k in range(4)]))
    a_real = placed[:, :width] + placed[:, width:2 * width]
    a_imag = placed[:, 2 * width:3 * width] + placed[:, 3 * width:]
    a_ref[:, :width] = a_real
    a_ref[:, width:] = a_imag
    inner = (row < F) & (col < F)
    modulus = jnp.where(inner, 0.0, jnp.sqrt(a_real * a_real + a_imag * a_imag))
    row_sums = jnp.sum(modulus, axis=1, keepdims=True)
    col_sums = jnp.sum(modulus, axis=0, keepdims=True)
    pa_ref[...] = lanes(a_real[:, :F], a_imag[:, :F])
    open_real = jnp.where(inner, 0.0, a_real)
    open_imag = jnp.where(inner, 0.0, a_imag)
    rh, rl = split(open_real)
    ih, il = split(open_imag)
    left = rows(lanes(rh, rh, rl, ih, ih, il), lanes(ih, ih, il, -rh, -rh, -rl))
    sk_ref[...] = mmt(left, lanes(rh, rl, rh, ih, il, ih))

    @pl.when(slab == 0)
    def _():
        b_ref[...] = lanes(jnp.zeros((F, F), f32), lead_ref[...])

    @pl.when(slab > 0)
    def _():
        forward.wait_recv()

    face = pa_ref[:F, :] - b_ref[...]
    pa_ref[:F, :] = face
    square = face * face
    face_mod = jnp.sqrt(square[:, :F] + square[:, F:])
    face_rows = jnp.sum(face_mod, axis=1, keepdims=True) + row_sums[:F]
    face_cols = jnp.sum(face_mod, axis=0, keepdims=True) + col_sums[:, :F]
    row_norm = jnp.maximum(jnp.max(row_sums[F:], axis=0, keepdims=True), jnp.max(face_rows, axis=0, keepdims=True))
    col_norm = jnp.maximum(jnp.max(col_sums[:, F:], axis=1, keepdims=True), jnp.max(face_cols, axis=1, keepdims=True))
    scale = 1.0 / (row_norm * col_norm)
    pa = pa_ref[...]
    other = swapped(face, 1.0, -1.0)
    ends = ends_ref[...]
    first = rows(face, other, lanes(ends, zero), lanes(zero, -ends))
    over = mmt(left3(first), right3(pa))
    down = mmt(left3(pa), right3(rows(face, -other)))
    inside = lax.broadcasted_iota(jnp.int32, (width, 2 * F), 1) < F
    below = (lax.broadcasted_iota(jnp.int32, (width, 2 * F), 0) >= F) & inside
    for part in range(2):
        base = part * width
        sk_ref[base:base + F, :] += over[part * F:(part + 1) * F]
        column = down if part == 0 else lanes(down[:, F:], down[:, :F])
        sk_ref[base:base + width, :2 * F] += jnp.where(below, column, 0.0)
    sym = unit - scale * sk_ref[:width, :]
    skew = -scale * sk_ref[width:, :]
    lr = scale * over[2 * F:3 * F]
    li = scale * over[3 * F:]

    for level in range(3):
        put(s_ref.at[level], sym)
        put(k_ref.at[level], skew)
        put(g_ref.at[level], sym + skew)
        put(t_ref.at[level], sym - skew)
        put(thin_ref.at[0], rows(lr, li))
        put(thin_ref.at[1], rows(-li, lr))
        weights = as_weights(s_ref.at[level], k_ref.at[level])
        grown = mm(lanes(tripled(g_ref.at[level]), tripled(t_ref.at[level])), weights)
        flipped = grown.T
        sym = 0.5 * (grown + flipped)
        skew = 0.5 * (grown - flipped)
        result = mm(lanes(tripled(thin_ref.at[0]), tripled(thin_ref.at[1])), weights)
        lr = lr + result[:F]
        li = li + result[F:]
    put(s_ref.at[3], sym)
    put(k_ref.at[3], skew)
    ur, ui = sym[:F], skew[:F]
    result = mm(
        lanes(left3(rows(lr, li, ur, ui)), left3(rows(-li, lr, -ui, ur))), as_weights(s_ref.at[3], k_ref.at[3])
    )
    w1r, w1i = ur + unit[:F], ui
    w2r, w2i = ur + result[2 * F:3 * F], ui + result[3 * F:]
    left = left3(lanes(lr, li, result[:F], result[F:2 * F]))
    right = right3(rows(lanes(w1r, w1i, w2r, w2i), lanes(-w1i, w1r, -w2i, w2r)))
    packed = mmt(left, right)
    both = rows(lanes(ends, zero), lanes(zero, ends))
    packed = mmt(left3(packed), right3(both))

    send_ref[...] = packed

    @pl.when(slab < last)
    def _():
        forward.start()

    @pl.when(slab == last)
    def _():
        for t in (3, 2, 4, 1, 5, 0, 6):
            messages[t].start()

    put(g_ref.at[3], sym + skew)
    put(t_ref.at[3], sym - skew)
    part_g = g_ref[0, 0].astype(f32) + g_ref[0, 1].astype(f32) + unit
    part_t = t_ref[0, 0].astype(f32) + t_ref[0, 1].astype(f32) + unit
    for level in range(1, 4):
        part_g = part_g + mm(lanes(left3(part_g), left3(part_t)), as_weights(s_ref.at[level], k_ref.at[level]))
        part_t = part_g.T
    grown = mm(lanes(tripled(g_ref.at[3]), tripled(t_ref.at[3])), as_weights(s_ref.at[3], k_ref.at[3]))
    flipped = grown.T
    highest = rows(right3v(0.5 * (grown + flipped)), right3v(0.5 * (grown - flipped)))
    part_g = part_g + mm(lanes(left3(part_g), left3(part_t)), highest)
    part_t = part_g.T
    pr = 0.5 * (part_g + part_t)
    pi = 0.5 * (part_g - part_t)
    a_ref[:F, :F] = face[:, :F]
    a_ref[:F, width:width + F] = face[:, F:]
    left = lanes(left3(a_ref[:, :width].T), left3(a_ref[:, width:].T))
    right = rows(right3v(lanes(pr, pi)), right3v(lanes(pi, -pr)))
    block = scale * mm(left, right)
    block_face = lanes(block[:F, :F], block[:F, width:width + F])
    face_all[slab] = block_face
    for t in (2, 1, 3, 0, 4, 5):
        @pl.when(face_goes(t))
        def _():
            give_face[t].start()

    hr, qr = split(block[:, :width])
    hi, qi = split(block[:, width:])
    turned = mm(perm_t_ref[...], lanes(hr, qr, hi, qi))
    back = turned.astype(bf16)
    back = mm(rows(*[back[:, k * width:(k + 1) * width] for k in range(4)]), perm)
    x_ref[0] = back[:width] + back[width:2 * width]
    x_ref[1] = back[2 * width:3 * width] + back[3 * width:]

    @pl.when(slab == last)
    def _():
        out_ref[0, 0, :, :, :] = x_ref[...]

    @pl.when(slab < last)
    def _():
        column = left3(
            lanes(
                turned[:, :F] + turned[:, width:width + F],
                turned[:, 2 * width:2 * width + F] + turned[:, 3 * width:3 * width + F],
            )
        )
        face_rows = mm(rows(hr[:F], qr[:F], hi[:F], qi[:F]), perm)
        rr = face_rows[:F] + face_rows[F:2 * F]
        ri = face_rows[2 * F:3 * F] + face_rows[3 * F:]
        across = across_of(rr, ri)
        one = unit[:F, :2 * F]
        part_ref[0] = jnp.zeros((F, 2 * F), f32)
        part_ref[1] = one
        part_ref[2] = one

        def compose(t, carry):
            remote(face_all.at[t], face_all.at[t], spread_sem.at[2, 0], face_sem.at[t], slab=slab).wait_recv()
            g = face_all[t]
            d = d_all[t - 1]
            both = right3(rows(lanes(d, zero), lanes(zero, d)))
            u = mm(left3(d), right3v(g))
            v = mmt(left3(g), both)
            k = mmt(left3(u), both)
            before, behind = part_ref[1], right3v(as_right(part_ref[2]))
            before = left3(before)
            part_ref[0] += mm(left3(mm(before, right3v(as_right(k)))), behind)
            part_ref[1] = mm(before, right3v(as_right(u)))
            part_ref[2] = mm(left3(v), behind)
            return carry

        lax.fori_loop(slab + 1, last, compose, 0)
        wide = mm(column, lanes(right3v(as_right(part_ref[0])), right3v(as_right(part_ref[1]))))
        more = mm(left3(wide[:, :2 * F]), across)
        x_ref[0] += more[:, :width]
        x_ref[1] += more[:, width:]
        column = left3(wide[:, 2 * F:])
        across = mm(left3(part_ref[2]), across_of(rr, ri))
        rr, ri = across[:, :width], across[:, width:]
        across = across_of(rr, ri)
        messages[0].wait_recv()
        incoming = right3v(as_right(m_ref[...]))
        more = mm(left3(mm(column, incoming)), across)
        out_ref[0, 0, 0, :, :] = x_ref[0] + more[:, :width]
        out_ref[0, 0, 1, :, :] = x_ref[1] + more[:, width:]

    @pl.when(slab < last)
    def _():
        forward.wait_send()

    @pl.when(slab == last)
    def _():
        for t in range(last):
            messages[t].wait_send()

    for t in range(slabs):
        @pl.when(d_goes(t))
        def _():
            give_d[t].wait_send()

        if t < last:
            @pl.when(face_goes(t))
            def _():
                give_face[t].wait_send()

    settle()


def run(energies, hamiltonian, coupling, green_prev, profile, phonon_weights, source, weight_index, left, right):
    width, faces = hamiltonian.shape[-1], coupling.shape[-1]
    slabs, lines = lax.axis_size("slab"), lax.axis_size("energy") // (NX * CORES)
    vmem, smem = pl.BlockSpec(memory_space=pltpu.VMEM), pl.BlockSpec(memory_space=pltpu.SMEM)
    face_block = pltpu.VMEM((faces, faces), f32)
    face_pair = pltpu.VMEM((faces, 2 * faces), f32)
    return pl.pallas_call(
        functools.partial(born_kernel, lines, slabs, width, faces),
        out_shape=jax.ShapeDtypeStruct((1, 1, 2, width, width), f32),
        in_specs=[smem] * 4 + [pl.BlockSpec(memory_space=pltpu.HBM)] * 6,
        out_specs=vmem,
        scratch_shapes=[
            pltpu.VMEM((2 * width, width), f32),
            pltpu.VMEM((width, width), f32),
            pltpu.VMEM((width, width), f32),
            face_block,
            pltpu.VMEM((1, faces), jnp.int32),
            pltpu.VMEM((1, faces), jnp.int32),
            pltpu.SemaphoreType.DMA((6,)),
        ] + EXCHANGE_SCRATCH(width) + [
            pltpu.VMEM((width, width), bf16),
            pltpu.VMEM((width, width), bf16),
            face_block,
            pltpu.VMEM((faces, faces), bf16),
            pltpu.VMEM((slabs, faces, faces), f32),
            pltpu.VMEM((slabs, faces, 2 * faces), f32),
            face_block, face_block,
            pltpu.VMEM((2 * width, width), f32),
            pltpu.VMEM((4, 2, width, width), bf16),
            pltpu.VMEM((4, 2, width, width), bf16),
            pltpu.VMEM((4, 2, width, width), bf16),
            pltpu.VMEM((4, 2, width, width), bf16),
            pltpu.VMEM((2, 2, 2 * faces, width), bf16),
            pltpu.VMEM((width, 2 * width), f32),
            face_pair, face_pair, face_pair,
            pltpu.VMEM((3, faces, 2 * faces), f32),
            pltpu.VMEM((width, 2 * faces), f32),
            pltpu.VMEM((2, width, width), f32),
            pltpu.SemaphoreType.DMA((2,)),
            pltpu.SemaphoreType.DMA((3,)),
            pltpu.SemaphoreType.DMA((3, slabs)),
            pltpu.SemaphoreType.DMA((slabs,)),
            pltpu.SemaphoreType.DMA((slabs,)),
            pltpu.SemaphoreType.REGULAR((3,)),
        ],
        compiler_params=pltpu.CompilerParams(
            collective_id=0, has_side_effects=True, vmem_limit_bytes=67043328
        ),
        name="born",
    )(
        energies, source, weight_index, phonon_weights,
        green_prev.reshape(2 * width, width), hamiltonian[0], profile, coupling[0], left, right,
    )


def solution(mesh):
    in_specs = (
        P("energy"),
        P("slab", None, None),
        P("slab", None, None),
        P("energy", "slab", None, None, None),
        P(),
        P(),
        P("energy", None),
        P("energy", None),
        P("slab", None),
        P("slab", None),
    )
    out_specs = P("energy", "slab", None, None, None)
    return jax.shard_map(run, mesh=mesh, in_specs=in_specs, out_specs=out_specs, check_vma=False)
```

```python
import functools
import jax
import jax.numpy as jnp
from jax import lax
from jax.experimental import pallas as pl
from jax.experimental.pallas import tpu as pltpu
from jax.sharding import PartitionSpec as P

BROAD = 0.02
f32 = jnp.float32
bf16 = jnp.bfloat16
MESH = pl.DeviceIdType.MESH


def mm(left, right):
    return jnp.dot(left, right, preferred_element_type=f32)


def mmt(left, right):
    return lax.dot_general(left, right, (((1,), (1,)), ((), ())), preferred_element_type=f32)


def split(value):
    high = value.astype(bf16)
    return high, (value - high.astype(f32)).astype(bf16)


def lanes(*pieces):
    return jnp.concatenate(pieces, axis=1)


def rows(*pieces):
    return jnp.concatenate(pieces, axis=0)


def left3(value):
    high, low = split(value)
    return lanes(high, high, low)


def right3(value):
    high, low = split(value)
    return lanes(high, low, high)


def right3v(value):
    high, low = split(value)
    return rows(high, low, high)


def swapped(packed, low_sign, high_sign):
    half = packed.shape[1] // 2
    lane = lax.broadcasted_iota(jnp.int32, packed.shape, 1)
    turned = lanes(packed[:, half:], packed[:, :half])
    return jnp.where(lane < half, low_sign * turned, high_sign * turned)


def put(ref, value):
    high, low = split(value)
    ref[0] = high
    ref[1] = low


def tripled(ref):
    return lanes(ref[0], ref[0], ref[1])


def as_weights(sym_ref, skew_ref):
    return rows(sym_ref[0], sym_ref[1], sym_ref[0], skew_ref[0], skew_ref[1], skew_ref[0])


def across_of(real, imag):
    return right3v(rows(lanes(real, imag), lanes(-imag, real)))


def as_right(packed):
    return rows(packed, swapped(packed, -1.0, 1.0))


NX = 4
CORES = 2
DEPTHS = (64,) * 8
CHUNKS = len(DEPTHS)
AHEAD = 3
FAR_LAG = 2
PARTNER_LAG = 3
LINE_LAG = 5
MEANWHILE = (1, 2, 3, 6)
FACTORS = (1.0, 2.0, 4.0, 16.0)
TABLE = 32


def where_on_energy():
    spot = lax.axis_index("energy")
    core = lax.rem(spot, CORES)
    chip = lax.div(spot, CORES)
    return lax.rem(chip, NX), lax.div(chip, NX), core


def energy_of(x, z, core):
    return (z * NX + x) * CORES + core


def remote(source, target, send, recv, **device):
    return pltpu.make_async_remote_copy(
        src_ref=source, dst_ref=target, send_sem=send, recv_sem=recv, device_id=device, device_id_type=MESH
    )


def greet(lines, slabs):
    x, z, core = where_on_energy()
    barrier = pltpu.get_barrier_semaphore()

    def signal(**device):
        pl.semaphore_signal(barrier, inc=1, device_id=device, device_id_type=MESH)

    signal(energy=energy_of(lax.rem(x + 1, NX), z, core))
    signal(energy=energy_of(lax.rem(x + NX - 1, NX), z, core))
    signal(energy=energy_of(x, z, 1 - core))
    count = 3
    for step, there in ((1, z < lines - 1), (-1, z > 0)):
        @pl.when(there)
        def _():
            signal(energy=energy_of(x, z + step, core))
            signal(energy=energy_of(x, z + step, 1 - core))
        count = count + 2 * there.astype(jnp.int32)
    if slabs > 1:
        slab = lax.axis_index("slab")
        for step in (1, slabs - 1):
            signal(slab=lax.rem(slab + step, slabs))
        count = count + 2
    return barrier, count


def make_table(source_ref, index_ref, weights_ref, table_ref):
    here = lax.axis_index("energy")
    row = lax.broadcasted_iota(jnp.int32, (TABLE, 128), 0)
    total = jnp.zeros((TABLE, 128), f32)
    for term in range(2):
        weight = weights_ref[index_ref[0, term]]
        distance = source_ref[0, term] - here + TABLE // 2
        total = total + jnp.where(row == distance, weight, 0.0)
    table_ref[0] = total


def exchange(lines, green, own, table_ref, got, part_send, part_recv, line_send, line_recv, acc,
             send_sem, recv_sem, table_send, table_recv, meanwhile, finish):
    x, z, core = where_on_energy()
    starts = [sum(DEPTHS[:q]) for q in range(CHUNKS)]
    right = energy_of(lax.rem(x + 1, NX), z, core)
    left = energy_of(lax.rem(x + NX - 1, NX), z, core)
    partner = energy_of(x, z, 1 - core)
    up_there, down_there = z < lines - 1, z > 0
    up, down = energy_of(x, z + 1, core), energy_of(x, z - 1, core)
    up_other, down_other = energy_of(x, z + 1, 1 - core), energy_of(x, z - 1, 1 - core)

    def span(chunk):
        return pl.ds(starts[chunk], DEPTHS[chunk])

    def part(ref, chunk):
        return ref.at[span(chunk), :]

    def tables(flow, device):
        return remote(table_ref.at[0], table_ref.at[flow + 1], table_send.at[flow], table_recv.at[flow], energy=device)

    to_partner = tables(0, partner)
    to_up, to_up_other = tables(3, up), tables(4, up_other)
    to_down, to_down_other = tables(1, down), tables(2, down_other)

    def piece(flow, chunk, source, target, device):
        return remote(source, target, send_sem.at[flow, chunk], recv_sem.at[flow, chunk], energy=device)

    to_right = [piece(0, q, part(green, q), part(got.at[0], q), right) for q in range(CHUNKS)]
    to_left = [piece(1, q, part(green, q), part(got.at[1], q), left) for q in range(CHUNKS)]
    onward = [
        piece(2, q, part(got.at[q % 2], q), part(got.at[2], q), right if q % 2 == 0 else left)
        for q in range(CHUNKS)
    ]
    across = [
        [piece(3 + k, q, part(part_send.at[k], q), part(part_recv.at[k], q), partner) for q in range(CHUNKS)]
        for k in range(3)
    ]
    upward = [piece(6, q, part(line_send.at[0], q), part(line_recv.at[0], q), up) for q in range(CHUNKS)]
    downward = [piece(7, q, part(line_send.at[1], q), part(line_recv.at[1], q), down) for q in range(CHUNKS)]

    def own_start(chunk):
        to_right[chunk].start()
        to_left[chunk].start()

    for chunk in range(AHEAD):
        own_start(chunk)
    to_partner.start()

    @pl.when(up_there)
    def _():
        to_up.start()
        to_up_other.start()

    @pl.when(down_there)
    def _():
        to_down.start()
        to_down_other.start()

    meanwhile[0]()
    to_partner.wait()

    @pl.when(up_there)
    def _():
        to_up.wait_send()
        to_up_other.wait_send()
        to_down.wait_recv()
        to_down_other.wait_recv()

    @pl.when(down_there)
    def _():
        to_down.wait_send()
        to_down_other.wait_send()
        to_up.wait_recv()
        to_up_other.wait_recv()

    apart = [0] + [lax.rem(x + step, NX) - x for step in (3, 1, 2)]

    def weighted(slot, line, other, chunk):
        total = None
        for k in range(4):
            lag = 2 * apart[k] + (2 * core - 1 if other else 0) - 8 * line + TABLE // 2
            weight = table_ref[slot, pl.ds(lag, 1), :]
            block = (own if k == 0 else got.at[k - 1])[span(chunk), :]
            term = lanes(weight, weight) * block
            total = term if total is None else total + term
        return total

    for step in range(CHUNKS + LINE_LAG):
        q = step
        if q < CHUNKS:
            to_right[q].wait_recv()
            to_left[q].wait_recv()
            onward[q].start()
            if q + AHEAD < CHUNKS:
                own_start(q + AHEAD)
        if step in MEANWHILE:
            meanwhile[1 + MEANWHILE.index(step)]()
        q = step - FAR_LAG
        if 0 <= q < CHUNKS:
            onward[q].wait_recv()
            piece_rows = span(q)
            acc[piece_rows, :] = weighted(0, 0, False, q)
            part_send[0, piece_rows, :] = weighted(1, 0, True, q)
            across[0][q].start()

            @pl.when(up_there)
            def _():
                line_send[0, piece_rows, :] = weighted(2, 1, False, q)
                part_send[1, piece_rows, :] = weighted(3, 1, True, q)
                across[1][q].start()

            @pl.when(down_there)
            def _():
                line_send[1, piece_rows, :] = weighted(4, -1, False, q)
                part_send[2, piece_rows, :] = weighted(5, -1, True, q)
                across[2][q].start()
        q = step - PARTNER_LAG
        if 0 <= q < CHUNKS:
            piece_rows = span(q)
            across[0][q].wait_recv()
            acc[piece_rows, :] += part_recv[0, piece_rows, :]

            @pl.when(up_there)
            def _():
                across[1][q].wait_recv()
                line_send[0, piece_rows, :] += part_recv[1, piece_rows, :]
                upward[q].start()

            @pl.when(down_there)
            def _():
                across[2][q].wait_recv()
                line_send[1, piece_rows, :] += part_recv[2, piece_rows, :]
                downward[q].start()
        q = step - LINE_LAG
        if 0 <= q < CHUNKS:
            piece_rows = span(q)

            @pl.when(down_there)
            def _():
                upward[q].wait_recv()
                acc[piece_rows, :] += line_recv[0, piece_rows, :]

            @pl.when(up_there)
            def _():
                downward[q].wait_recv()
                acc[piece_rows, :] += line_recv[1, piece_rows, :]

            finish(starts[q], DEPTHS[q])

    def settle():
        for q in range(CHUNKS):
            to_right[q].wait_send()
            to_left[q].wait_send()
            onward[q].wait_send()
            across[0][q].wait_send()

            @pl.when(up_there)
            def _():
                across[1][q].wait_send()
                upward[q].wait_send()

            @pl.when(down_there)
            def _():
                across[2][q].wait_send()
                downward[q].wait_send()

    return settle


EXCHANGE_SCRATCH = lambda width: [
    pltpu.VMEM((6, TABLE, 128), f32),
    pltpu.VMEM((3, 2 * width, width), f32),
    pltpu.VMEM((3, 2 * width, width), f32),
    pltpu.VMEM((3, 2 * width, width), f32),
    pltpu.VMEM((2, 2 * width, width), f32),
    pltpu.VMEM((2, 2 * width, width), f32),
    pltpu.VMEM((2 * width, width), f32),
    pltpu.SemaphoreType.DMA((8, CHUNKS)),
    pltpu.SemaphoreType.DMA((8, CHUNKS)),
    pltpu.SemaphoreType.DMA((5,)),
    pltpu.SemaphoreType.DMA((5,)),
]


def born_kernel(
    lines, slabs, width, faces,
    energy_ref, source_ref, index_ref, weights_ref, green_in, ham_in, profile_in, coup_in, left_in, right_in,
    out_ref,
    green_ref, ham_ref, profile_ref, coup_ref, left_ref, right_ref, load_sem,
    table_ref, got, part_send, part_recv, line_send, line_recv, acc, piece_send, piece_recv, table_send, table_recv,
    perm_ref, perm_t_ref, next_ref, order_ref, d_all, face_all, ends_ref, lead_ref,
    sk_ref, g_ref, t_ref, s_ref, k_ref, thin_ref, a_ref, b_ref, m_ref, send_ref, part_ref, pa_ref, x_ref,
    send_sem, recv_sem, spread_sem, d_sem, face_sem, known_sem,
):
    slab = lax.axis_index("slab")
    F = faces
    row = lax.broadcasted_iota(jnp.int32, (width, width), 0)
    col = lax.broadcasted_iota(jnp.int32, (width, width), 1)
    unit = jnp.where(row == col, 1.0, 0.0)
    barrier, greetings = greet(lines, slabs)
    loads = [
        pltpu.make_async_copy(source, target, load_sem.at[k])
        for k, (source, target) in enumerate((
            (coup_in, coup_ref), (left_in, left_ref), (right_in, right_ref),
            (green_in, green_ref), (ham_in, ham_ref), (profile_in, profile_ref),
        ))
    ]
    for load in loads:
        load.start()
    make_table(source_ref, index_ref, weights_ref, table_ref)
    pl.semaphore_wait(barrier, greetings)
    last = slabs - 1
    forward = remote(send_ref, b_ref, send_sem.at[0], recv_sem.at[0], slab=lax.rem(slab + 1, slabs))
    give_coupling = remote(coup_ref, next_ref, send_sem.at[1], recv_sem.at[1], slab=lax.rem(slab + last, slabs))
    messages = [remote(send_ref, m_ref, spread_sem.at[0, t], recv_sem.at[2], slab=t) for t in range(last)]
    give_d = [
        remote(d_all.at[slab], d_all.at[slab], spread_sem.at[1, t], d_sem.at[slab], slab=t) for t in range(slabs)
    ]
    give_face = [
        remote(face_all.at[slab], face_all.at[slab], spread_sem.at[2, t], face_sem.at[slab], slab=t)
        for t in range(last)
    ]

    def d_goes(t):
        return (slab == last - 1) if t == last else ((slab > t) & (slab < last - 1))

    def face_goes(t):
        return (slab > t) & (slab < last)

    zero = jnp.zeros((F, F), f32)

    def tell(hop):
        for step in (1, last):
            pl.semaphore_signal(
                known_sem.at[hop], inc=1, device_id={"slab": lax.rem(slab + step, slabs)}, device_id_type=MESH
            )

    def first_stage():
        tell(0)
        for load in loads:
            load.wait()
        give_coupling.start()
        spot = lax.broadcasted_iota(jnp.int32, (width, F), 0)
        hot_left = jnp.where(spot == left_ref[...], 1.0, 0.0)
        hot_right = jnp.where(spot == right_ref[...], 1.0, 0.0)
        on_face = jnp.sum(hot_left, axis=1, keepdims=True)
        off_face = jnp.broadcast_to(1.0 - on_face, (width, 128)).astype(bf16)
        before = mm(jnp.where(col < row, 1.0, 0.0).astype(bf16), off_face)[:, :1]
        rest = jnp.where(col == F + before.astype(jnp.int32), 1.0 - on_face, 0.0)
        perm_t = rest + lanes(hot_left, jnp.zeros((width, width - F), f32))
        perm_t_ref[...] = perm_t.astype(bf16)
        perm_ref[...] = perm_t.T.astype(bf16)
        order_ref[...] = mm(hot_left.T.astype(bf16), hot_right.astype(bf16)).astype(bf16)
        coup = coup_ref[...]
        lead_ref[...] = -0.5 * mm(left3(coup.T), right3v(coup))

    def hear_stage():
        pl.semaphore_wait(known_sem.at[0], 2)
        tell(1)

    def second_stage():
        pl.semaphore_wait(known_sem.at[1], 2)
        tell(2)
        give_coupling.wait()
        following = next_ref[...]
        high, low = split(following)
        lowest = (following - high.astype(f32) - low.astype(f32)).astype(bf16)
        order = order_ref[...]
        here = mm(lanes(order, order, order), rows(high, low, lowest))
        d_all[slab] = here
        ends_ref[...] = here.T

    def spread_stage():
        pl.semaphore_wait(known_sem.at[2], 2)
        for t in range(slabs):
            @pl.when(d_goes(t))
            def _():
                give_d[t].start()

    def third_stage():
        def arrived(t, carry):
            remote(d_all.at[t], d_all.at[t], spread_sem.at[1, 0], d_sem.at[t], slab=slab).wait_recv()
            return carry

        lax.fori_loop(slab + 1, last - 1, arrived, 0)

        @pl.when(slab == last)
        def _():
            arrived(last - 1, 0)
            ends_ref[...] = d_all[last - 1]

    def finish(first, depth):
        piece_rows = pl.ds(first, depth)
        imag = first >= width
        there = pl.ds(first - width if imag else first, depth)
        diagonal = jnp.where(
            lax.broadcasted_iota(jnp.int32, (depth, width), 0) + (first - width if imag else first)
            == lax.broadcasted_iota(jnp.int32, (depth, width), 1),
            1.0, 0.0,
        )
        sigma = profile_ref[there, :] * acc[piece_rows, :]
        if imag:
            acc[piece_rows, :] = BROAD * diagonal - sigma
        else:
            acc[piece_rows, :] = energy_ref[0] * diagonal - ham_ref[there, :] - sigma

    settle = exchange(lines, green_in, green_ref, table_ref, got, part_send, part_recv, line_send, line_recv, acc,
                      piece_send, piece_recv, table_send, table_recv,
                      (first_stage, hear_stage, second_stage, spread_stage, third_stage), finish)

    perm = perm_ref[...]
    pieces = split(acc[:width, :]) + split(acc[width:, :])
    turned = mmt(rows(*pieces), perm).astype(bf16)
    placed = mm(perm, lanes(*[turned[k * width:(k + 1) * width] for k in range(4)]))
    a_real = placed[:, :width] + placed[:, width:2 * width]
    a_imag = placed[:, 2 * width:3 * width] + placed[:, 3 * width:]
    a_ref[:, :width] = a_real
    a_ref[:, width:] = a_imag
    inner = (row < F) & (col < F)
    modulus = jnp.where(inner, 0.0, jnp.sqrt(a_real * a_real + a_imag * a_imag))
    row_sums = jnp.sum(modulus, axis=1, keepdims=True)
    col_sums = jnp.sum(modulus, axis=0, keepdims=True)
    pa_ref[...] = lanes(a_real[:, :F], a_imag[:, :F])
    open_real = jnp.where(inner, 0.0, a_real)
    open_imag = jnp.where(inner, 0.0, a_imag)
    rh, rl = split(open_real)
    ih, il = split(open_imag)
    left = rows(lanes(rh, rh, rl, ih, ih, il), lanes(ih, ih, il, -rh, -rh, -rl))
    sk_ref[...] = mmt(left, lanes(rh, rl, rh, ih, il, ih))

    @pl.when(slab == 0)
    def _():
        b_ref[...] = lanes(jnp.zeros((F, F), f32), lead_ref[...])

    @pl.when(slab > 0)
    def _():
        forward.wait_recv()

    face = pa_ref[:F, :] - b_ref[...]
    pa_ref[:F, :] = face
    square = face * face
    face_mod = jnp.sqrt(square[:, :F] + square[:, F:])
    face_rows = jnp.sum(face_mod, axis=1, keepdims=True) + row_sums[:F]
    face_cols = jnp.sum(face_mod, axis=0, keepdims=True) + col_sums[:, :F]
    row_norm = jnp.maximum(jnp.max(row_sums[F:], axis=0, keepdims=True), jnp.max(face_rows, axis=0, keepdims=True))
    col_norm = jnp.maximum(jnp.max(col_sums[:, F:], axis=1, keepdims=True), jnp.max(face_cols, axis=1, keepdims=True))
    scale = 1.0 / (row_norm * col_norm)
    pa = pa_ref[...]
    other = swapped(face, 1.0, -1.0)
    ends = ends_ref[...]
    first = rows(face, other, lanes(ends, zero), lanes(zero, -ends))
    over = mmt(left3(first), right3(pa))
    down = mmt(left3(pa), right3(rows(face, -other)))
    inside = lax.broadcasted_iota(jnp.int32, (width, 2 * F), 1) < F
    below = (lax.broadcasted_iota(jnp.int32, (width, 2 * F), 0) >= F) & inside
    for part in range(2):
        base = part * width
        sk_ref[base:base + F, :] += over[part * F:(part + 1) * F]
        column = down if part == 0 else lanes(down[:, F:], down[:, :F])
        sk_ref[base:base + width, :2 * F] += jnp.where(below, column, 0.0)
    sym = unit - scale * sk_ref[:width, :]
    skew = -scale * sk_ref[width:, :]
    lr = scale * over[2 * F:3 * F]
    li = scale * over[3 * F:]

    def thin(level, real, imag):
        put(thin_ref.at[0], rows(real, imag))
        put(thin_ref.at[1], rows(-imag, real))
        product = mm(
            lanes(tripled(thin_ref.at[0]), tripled(thin_ref.at[1])), as_weights(s_ref.at[level], k_ref.at[level])
        )
        return product * (1.0 / FACTORS[level])

    grown, flipped = sym + skew, sym - skew
    for level in range(3):
        put(s_ref.at[level], sym)
        put(k_ref.at[level], skew)
        put(g_ref.at[level], grown)
        put(t_ref.at[level], flipped)
        grown = mm(
            lanes(tripled(g_ref.at[level]), tripled(t_ref.at[level])), as_weights(s_ref.at[level], k_ref.at[level])
        )
        result = thin(level, lr, li)
        lr = lr + result[:F]
        li = li + result[F:]
        flipped = grown.T
        sym = grown + flipped
        skew = grown - flipped
    put(s_ref.at[3], sym)
    put(k_ref.at[3], skew)
    ur, ui = sym[:F] * (1.0 / FACTORS[3]), skew[:F] * (1.0 / FACTORS[3])
    upper = mm(
        lanes(left3(rows(ur, ui)), left3(rows(-ui, ur))), as_weights(s_ref.at[3], k_ref.at[3])
    ) * (1.0 / FACTORS[3])
    result = rows(thin(3, lr, li), upper)
    w1r, w1i = ur + unit[:F], ui
    w2r, w2i = ur + result[2 * F:3 * F], ui + result[3 * F:]
    left = left3(lanes(lr, li, result[:F], result[F:2 * F]))
    right = right3(rows(lanes(w1r, w1i, w2r, w2i), lanes(-w1i, w1r, -w2i, w2r)))
    packed = mmt(left, right)
    both = rows(lanes(ends, zero), lanes(zero, ends))
    packed = mmt(left3(packed), right3(both))

    send_ref[...] = packed

    @pl.when(slab < last)
    def _():
        forward.start()

    @pl.when(slab == last)
    def _():
        for t in (3, 2, 4, 1, 5, 0, 6):
            messages[t].start()

    put(g_ref.at[3], grown)
    put(t_ref.at[3], flipped)
    part_g = g_ref[0, 0].astype(f32) + g_ref[0, 1].astype(f32) + unit
    part_t = t_ref[0, 0].astype(f32) + t_ref[0, 1].astype(f32) + unit
    for level in range(1, 4):
        part_g = part_g + mm(lanes(left3(part_g), left3(part_t)), as_weights(s_ref.at[level], k_ref.at[level])) * (
            1.0 / FACTORS[level]
        )
        part_t = part_g.T
    grown = mm(lanes(tripled(g_ref.at[3]), tripled(t_ref.at[3])), as_weights(s_ref.at[3], k_ref.at[3]))
    flipped = grown.T
    half = 0.5 * FACTORS[1] / (FACTORS[3] * FACTORS[3])
    highest = rows(right3v(half * (grown + flipped)), right3v(half * (grown - flipped)))
    part_g = part_g + mm(lanes(left3(part_g), left3(part_t)), highest)
    part_t = part_g.T
    pr = 0.5 * (part_g + part_t)
    pi = 0.5 * (part_g - part_t)
    a_ref[:F, :F] = face[:, :F]
    a_ref[:F, width:width + F] = face[:, F:]
    left = lanes(left3(a_ref[:, :width].T), left3(a_ref[:, width:].T))
    right = rows(right3v(lanes(pr, pi)), right3v(lanes(pi, -pr)))
    block = scale * mm(left, right)
    block_face = lanes(block[:F, :F], block[:F, width:width + F])
    face_all[slab] = block_face
    for t in (2, 1, 3, 0, 4, 5):
        @pl.when(face_goes(t))
        def _():
            give_face[t].start()

    hr, qr = split(block[:, :width])
    hi, qi = split(block[:, width:])
    turned = mm(perm_t_ref[...], lanes(hr, qr, hi, qi))
    back = turned.astype(bf16)
    back = mm(rows(*[back[:, k * width:(k + 1) * width] for k in range(4)]), perm)
    x_ref[0] = back[:width] + back[width:2 * width]
    x_ref[1] = back[2 * width:3 * width] + back[3 * width:]

    @pl.when(slab == last)
    def _():
        out_ref[0, 0, :, :, :] = x_ref[...]

    @pl.when(slab < last)
    def _():
        column = left3(
            lanes(
                turned[:, :F] + turned[:, width:width + F],
                turned[:, 2 * width:2 * width + F] + turned[:, 3 * width:3 * width + F],
            )
        )
        face_rows = mm(rows(hr[:F], qr[:F], hi[:F], qi[:F]), perm)
        rr = face_rows[:F] + face_rows[F:2 * F]
        ri = face_rows[2 * F:3 * F] + face_rows[3 * F:]
        across = across_of(rr, ri)
        one = unit[:F, :2 * F]
        part_ref[0] = jnp.zeros((F, 2 * F), f32)
        part_ref[1] = one
        part_ref[2] = one

        def compose(t, carry):
            remote(face_all.at[t], face_all.at[t], spread_sem.at[2, 0], face_sem.at[t], slab=slab).wait_recv()
            g = face_all[t]
            d = d_all[t - 1]
            both = right3(rows(lanes(d, zero), lanes(zero, d)))
            u = mm(left3(d), right3v(g))
            v = mmt(left3(g), both)
            k = mmt(left3(u), both)
            before, behind = part_ref[1], right3v(as_right(part_ref[2]))
            before = left3(before)
            part_ref[0] += mm(left3(mm(before, right3v(as_right(k)))), behind)
            part_ref[1] = mm(before, right3v(as_right(u)))
            part_ref[2] = mm(left3(v), behind)
            return carry

        lax.fori_loop(slab + 1, last, compose, 0)
        wide = mm(column, lanes(right3v(as_right(part_ref[0])), right3v(as_right(part_ref[1]))))
        more = mm(left3(wide[:, :2 * F]), across)
        x_ref[0] += more[:, :width]
        x_ref[1] += more[:, width:]
        column = left3(wide[:, 2 * F:])
        across = mm(left3(part_ref[2]), across_of(rr, ri))
        rr, ri = across[:, :width], across[:, width:]
        across = across_of(rr, ri)
        messages[0].wait_recv()
        incoming = right3v(as_right(m_ref[...]))
        more = mm(left3(mm(column, incoming)), across)
        out_ref[0, 0, 0, :, :] = x_ref[0] + more[:, :width]
        out_ref[0, 0, 1, :, :] = x_ref[1] + more[:, width:]

    @pl.when(slab < last)
    def _():
        forward.wait_send()

    @pl.when(slab == last)
    def _():
        for t in range(last):
            messages[t].wait_send()

    for t in range(slabs):
        @pl.when(d_goes(t))
        def _():
            give_d[t].wait_send()

        if t < last:
            @pl.when(face_goes(t))
            def _():
                give_face[t].wait_send()

    settle()


def run(energies, hamiltonian, coupling, green_prev, profile, phonon_weights, source, weight_index, left, right):
    width, faces = hamiltonian.shape[-1], coupling.shape[-1]
    slabs, lines = lax.axis_size("slab"), lax.axis_size("energy") // (NX * CORES)
    vmem, smem = pl.BlockSpec(memory_space=pltpu.VMEM), pl.BlockSpec(memory_space=pltpu.SMEM)
    face_block = pltpu.VMEM((faces, faces), f32)
    face_pair = pltpu.VMEM((faces, 2 * faces), f32)
    return pl.pallas_call(
        functools.partial(born_kernel, lines, slabs, width, faces),
        out_shape=jax.ShapeDtypeStruct((1, 1, 2, width, width), f32),
        in_specs=[smem] * 4 + [pl.BlockSpec(memory_space=pltpu.HBM)] * 6,
        out_specs=vmem,
        scratch_shapes=[
            pltpu.VMEM((2 * width, width), f32),
            pltpu.VMEM((width, width), f32),
            pltpu.VMEM((width, width), f32),
            face_block,
            pltpu.VMEM((1, faces), jnp.int32),
            pltpu.VMEM((1, faces), jnp.int32),
            pltpu.SemaphoreType.DMA((6,)),
        ] + EXCHANGE_SCRATCH(width) + [
            pltpu.VMEM((width, width), bf16),
            pltpu.VMEM((width, width), bf16),
            face_block,
            pltpu.VMEM((faces, faces), bf16),
            pltpu.VMEM((slabs, faces, faces), f32),
            pltpu.VMEM((slabs, faces, 2 * faces), f32),
            face_block, face_block,
            pltpu.VMEM((2 * width, width), f32),
            pltpu.VMEM((4, 2, width, width), bf16),
            pltpu.VMEM((4, 2, width, width), bf16),
            pltpu.VMEM((4, 2, width, width), bf16),
            pltpu.VMEM((4, 2, width, width), bf16),
            pltpu.VMEM((2, 2, 2 * faces, width), bf16),
            pltpu.VMEM((width, 2 * width), f32),
            face_pair, face_pair, face_pair,
            pltpu.VMEM((3, faces, 2 * faces), f32),
            pltpu.VMEM((width, 2 * faces), f32),
            pltpu.VMEM((2, width, width), f32),
            pltpu.SemaphoreType.DMA((2,)),
            pltpu.SemaphoreType.DMA((3,)),
            pltpu.SemaphoreType.DMA((3, slabs)),
            pltpu.SemaphoreType.DMA((slabs,)),
            pltpu.SemaphoreType.DMA((slabs,)),
            pltpu.SemaphoreType.REGULAR((3,)),
        ],
        compiler_params=pltpu.CompilerParams(
            collective_id=0, has_side_effects=True, vmem_limit_bytes=67043328
        ),
        name="born",
    )(
        energies, source, weight_index, phonon_weights,
        green_prev.reshape(2 * width, width), hamiltonian[0], profile, coupling[0], left, right,
    )


def solution(mesh):
    in_specs = (
        P("energy"),
        P("slab", None, None),
        P("slab", None, None),
        P("energy", "slab", None, None, None),
        P(),
        P(),
        P("energy", None),
        P("energy", None),
        P("slab", None),
        P("slab", None),
    )
    out_specs = P("energy", "slab", None, None, None)
    return jax.shard_map(run, mesh=mesh, in_specs=in_specs, out_specs=out_specs, check_vma=False)
```

```python
import functools
import jax
import jax.numpy as jnp
from jax import lax
from jax.experimental import pallas as pl
from jax.experimental.pallas import tpu as pltpu
from jax.sharding import PartitionSpec as P

BROAD = 0.02
f32 = jnp.float32
bf16 = jnp.bfloat16
MESH = pl.DeviceIdType.MESH


def mm(left, right):
    return jnp.dot(left, right, preferred_element_type=f32)


def mmt(left, right):
    return lax.dot_general(left, right, (((1,), (1,)), ((), ())), preferred_element_type=f32)


def by_halves(left, right):
    half = left.shape[0] // 2
    return rows(mm(left[:half], right), mm(left[half:], right))


def split(value):
    high = value.astype(bf16)
    return high, (value - high.astype(f32)).astype(bf16)


def lanes(*pieces):
    return jnp.concatenate(pieces, axis=1)


def rows(*pieces):
    return jnp.concatenate(pieces, axis=0)


def left3(value):
    high, low = split(value)
    return lanes(high, high, low)


def right3(value):
    high, low = split(value)
    return lanes(high, low, high)


def right3v(value):
    high, low = split(value)
    return rows(high, low, high)


def swapped(packed, low_sign, high_sign):
    half = packed.shape[1] // 2
    lane = lax.broadcasted_iota(jnp.int32, packed.shape, 1)
    turned = lanes(packed[:, half:], packed[:, :half])
    return jnp.where(lane < half, low_sign * turned, high_sign * turned)


def put(ref, value):
    high, low = split(value)
    ref[0] = high
    ref[1] = low


def tripled(ref):
    return lanes(ref[0], ref[0], ref[1])


def as_weights(sym_ref, skew_ref):
    return rows(sym_ref[0], sym_ref[1], sym_ref[0], skew_ref[0], skew_ref[1], skew_ref[0])


def across_of(real, imag):
    return right3v(rows(lanes(real, imag), lanes(-imag, real)))


def as_right(packed):
    return rows(packed, swapped(packed, -1.0, 1.0))


NX = 4
CORES = 2
DEPTHS = (64,) * 8
CHUNKS = len(DEPTHS)
AHEAD = 3
FAR_LAG = 2
PARTNER_LAG = 3
LINE_LAG = 5
MEANWHILE = (1, 2, 3, 6)
FACTORS = (1.0, 2.0, 4.0, 16.0)
TABLE = 32


def where_on_energy():
    spot = lax.axis_index("energy")
    core = lax.rem(spot, CORES)
    chip = lax.div(spot, CORES)
    return lax.rem(chip, NX), lax.div(chip, NX), core


def energy_of(x, z, core):
    return (z * NX + x) * CORES + core


def remote(source, target, send, recv, **device):
    return pltpu.make_async_remote_copy(
        src_ref=source, dst_ref=target, send_sem=send, recv_sem=recv, device_id=device, device_id_type=MESH
    )


def greet(lines, slabs):
    x, z, core = where_on_energy()
    barrier = pltpu.get_barrier_semaphore()

    def signal(**device):
        pl.semaphore_signal(barrier, inc=1, device_id=device, device_id_type=MESH)

    signal(energy=energy_of(lax.rem(x + 1, NX), z, core))
    signal(energy=energy_of(lax.rem(x + NX - 1, NX), z, core))
    signal(energy=energy_of(x, z, 1 - core))
    count = 3
    for step, there in ((1, z < lines - 1), (-1, z > 0)):
        @pl.when(there)
        def _():
            signal(energy=energy_of(x, z + step, core))
            signal(energy=energy_of(x, z + step, 1 - core))
        count = count + 2 * there.astype(jnp.int32)
    if slabs > 1:
        slab = lax.axis_index("slab")
        for step in (1, slabs - 1):
            signal(slab=lax.rem(slab + step, slabs))
        count = count + 2
    return barrier, count


def make_table(source_ref, index_ref, weights_ref, table_ref):
    here = lax.axis_index("energy")
    row = lax.broadcasted_iota(jnp.int32, (TABLE, 128), 0)
    total = jnp.zeros((TABLE, 128), f32)
    for term in range(2):
        weight = weights_ref[index_ref[0, term]]
        distance = source_ref[0, term] - here + TABLE // 2
        total = total + jnp.where(row == distance, weight, 0.0)
    table_ref[0] = total


def exchange(lines, green, own, table_ref, got, part_send, part_recv, line_send, line_recv, acc,
             send_sem, recv_sem, table_send, table_recv, meanwhile, finish):
    x, z, core = where_on_energy()
    starts = [sum(DEPTHS[:q]) for q in range(CHUNKS)]
    right = energy_of(lax.rem(x + 1, NX), z, core)
    left = energy_of(lax.rem(x + NX - 1, NX), z, core)
    partner = energy_of(x, z, 1 - core)
    up_there, down_there = z < lines - 1, z > 0
    up, down = energy_of(x, z + 1, core), energy_of(x, z - 1, core)
    up_other, down_other = energy_of(x, z + 1, 1 - core), energy_of(x, z - 1, 1 - core)

    def span(chunk):
        return pl.ds(starts[chunk], DEPTHS[chunk])

    def part(ref, chunk):
        return ref.at[span(chunk), :]

    def tables(flow, device):
        return remote(table_ref.at[0], table_ref.at[flow + 1], table_send.at[flow], table_recv.at[flow], energy=device)

    to_partner = tables(0, partner)
    to_up, to_up_other = tables(3, up), tables(4, up_other)
    to_down, to_down_other = tables(1, down), tables(2, down_other)

    def piece(flow, chunk, source, target, device):
        return remote(source, target, send_sem.at[flow, chunk], recv_sem.at[flow, chunk], energy=device)

    to_right = [piece(0, q, part(green, q), part(got.at[0], q), right) for q in range(CHUNKS)]
    to_left = [piece(1, q, part(green, q), part(got.at[1], q), left) for q in range(CHUNKS)]
    onward = [
        piece(2, q, part(got.at[q % 2], q), part(got.at[2], q), right if q % 2 == 0 else left)
        for q in range(CHUNKS)
    ]
    across = [
        [piece(3 + k, q, part(part_send.at[k], q), part(part_recv.at[k], q), partner) for q in range(CHUNKS)]
        for k in range(3)
    ]
    upward = [piece(6, q, part(line_send.at[0], q), part(line_recv.at[0], q), up) for q in range(CHUNKS)]
    downward = [piece(7, q, part(line_send.at[1], q), part(line_recv.at[1], q), down) for q in range(CHUNKS)]

    def own_start(chunk):
        to_right[chunk].start()
        to_left[chunk].start()

    for chunk in range(AHEAD):
        own_start(chunk)
    to_partner.start()

    @pl.when(up_there)
    def _():
        to_up.start()
        to_up_other.start()

    @pl.when(down_there)
    def _():
        to_down.start()
        to_down_other.start()

    meanwhile[0]()
    to_partner.wait()

    @pl.when(up_there)
    def _():
        to_up.wait_send()
        to_up_other.wait_send()
        to_down.wait_recv()
        to_down_other.wait_recv()

    @pl.when(down_there)
    def _():
        to_down.wait_send()
        to_down_other.wait_send()
        to_up.wait_recv()
        to_up_other.wait_recv()

    apart = [0] + [lax.rem(x + step, NX) - x for step in (3, 1, 2)]

    def weighted(slot, line, other, chunk):
        total = None
        for k in range(4):
            lag = 2 * apart[k] + (2 * core - 1 if other else 0) - 8 * line + TABLE // 2
            weight = table_ref[slot, pl.ds(lag, 1), :]
            block = (own if k == 0 else got.at[k - 1])[span(chunk), :]
            term = lanes(weight, weight) * block
            total = term if total is None else total + term
        return total

    for step in range(CHUNKS + LINE_LAG):
        q = step
        if q < CHUNKS:
            to_right[q].wait_recv()
            to_left[q].wait_recv()
            onward[q].start()
            if q + AHEAD < CHUNKS:
                own_start(q + AHEAD)
        if step in MEANWHILE:
            meanwhile[1 + MEANWHILE.index(step)]()
        q = step - FAR_LAG
        if 0 <= q < CHUNKS:
            onward[q].wait_recv()
            piece_rows = span(q)
            acc[piece_rows, :] = weighted(0, 0, False, q)
            part_send[0, piece_rows, :] = weighted(1, 0, True, q)
            across[0][q].start()

            @pl.when(up_there)
            def _():
                line_send[0, piece_rows, :] = weighted(2, 1, False, q)
                part_send[1, piece_rows, :] = weighted(3, 1, True, q)
                across[1][q].start()

            @pl.when(down_there)
            def _():
                line_send[1, piece_rows, :] = weighted(4, -1, False, q)
                part_send[2, piece_rows, :] = weighted(5, -1, True, q)
                across[2][q].start()
        q = step - PARTNER_LAG
        if 0 <= q < CHUNKS:
            piece_rows = span(q)
            across[0][q].wait_recv()
            acc[piece_rows, :] += part_recv[0, piece_rows, :]

            @pl.when(up_there)
            def _():
                across[1][q].wait_recv()
                line_send[0, piece_rows, :] += part_recv[1, piece_rows, :]
                upward[q].start()

            @pl.when(down_there)
            def _():
                across[2][q].wait_recv()
                line_send[1, piece_rows, :] += part_recv[2, piece_rows, :]
                downward[q].start()
        q = step - LINE_LAG
        if 0 <= q < CHUNKS:
            piece_rows = span(q)

            @pl.when(down_there)
            def _():
                upward[q].wait_recv()
                acc[piece_rows, :] += line_recv[0, piece_rows, :]

            @pl.when(up_there)
            def _():
                downward[q].wait_recv()
                acc[piece_rows, :] += line_recv[1, piece_rows, :]

            finish(starts[q], DEPTHS[q])

    def settle():
        for q in range(CHUNKS):
            to_right[q].wait_send()
            to_left[q].wait_send()
            onward[q].wait_send()
            across[0][q].wait_send()

            @pl.when(up_there)
            def _():
                across[1][q].wait_send()
                upward[q].wait_send()

            @pl.when(down_there)
            def _():
                across[2][q].wait_send()
                downward[q].wait_send()

    return settle


EXCHANGE_SCRATCH = lambda width: [
    pltpu.VMEM((6, TABLE, 128), f32),
    pltpu.VMEM((3, 2 * width, width), f32),
    pltpu.VMEM((3, 2 * width, width), f32),
    pltpu.VMEM((3, 2 * width, width), f32),
    pltpu.VMEM((2, 2 * width, width), f32),
    pltpu.VMEM((2, 2 * width, width), f32),
    pltpu.VMEM((2 * width, width), f32),
    pltpu.SemaphoreType.DMA((8, CHUNKS)),
    pltpu.SemaphoreType.DMA((8, CHUNKS)),
    pltpu.SemaphoreType.DMA((5,)),
    pltpu.SemaphoreType.DMA((5,)),
]


def born_kernel(
    lines, slabs, width, faces,
    energy_ref, source_ref, index_ref, weights_ref, green_in, ham_in, profile_in, coup_in, left_in, right_in,
    out_ref,
    green_ref, ham_ref, profile_ref, coup_ref, left_ref, right_ref, load_sem,
    table_ref, got, part_send, part_recv, line_send, line_recv, acc, piece_send, piece_recv, table_send, table_recv,
    perm_ref, perm_t_ref, next_ref, order_ref, d_all, face_all, ends_ref, lead_ref,
    sk_ref, g_ref, t_ref, s_ref, k_ref, thin_ref, a_ref, b_ref, m_ref, send_ref, part_ref, pa_ref, x_ref,
    send_sem, recv_sem, spread_sem, d_sem, face_sem, known_sem,
):
    slab = lax.axis_index("slab")
    F = faces
    row = lax.broadcasted_iota(jnp.int32, (width, width), 0)
    col = lax.broadcasted_iota(jnp.int32, (width, width), 1)
    unit = jnp.where(row == col, 1.0, 0.0)
    barrier, greetings = greet(lines, slabs)
    loads = [
        pltpu.make_async_copy(source, target, load_sem.at[k])
        for k, (source, target) in enumerate((
            (coup_in, coup_ref), (left_in, left_ref), (right_in, right_ref),
            (green_in, green_ref), (ham_in, ham_ref), (profile_in, profile_ref),
        ))
    ]
    for load in loads:
        load.start()
    make_table(source_ref, index_ref, weights_ref, table_ref)
    pl.semaphore_wait(barrier, greetings)
    last = slabs - 1
    forward = remote(send_ref, b_ref, send_sem.at[0], recv_sem.at[0], slab=lax.rem(slab + 1, slabs))
    give_coupling = remote(coup_ref, next_ref, send_sem.at[1], recv_sem.at[1], slab=lax.rem(slab + last, slabs))
    messages = [remote(send_ref, m_ref, spread_sem.at[0, t], recv_sem.at[2], slab=t) for t in range(last)]
    give_d = [
        remote(d_all.at[slab], d_all.at[slab], spread_sem.at[1, t], d_sem.at[slab], slab=t) for t in range(slabs)
    ]
    give_face = [
        remote(face_all.at[slab], face_all.at[slab], spread_sem.at[2, t], face_sem.at[slab], slab=t)
        for t in range(last)
    ]

    def d_goes(t):
        return (slab == last - 1) if t == last else ((slab > t) & (slab < last - 1))

    def face_goes(t):
        return (slab > t) & (slab < last)

    zero = jnp.zeros((F, F), f32)

    def tell(hop):
        for step in (1, last):
            pl.semaphore_signal(
                known_sem.at[hop], inc=1, device_id={"slab": lax.rem(slab + step, slabs)}, device_id_type=MESH
            )

    def first_stage():
        tell(0)
        for load in loads:
            load.wait()
        give_coupling.start()
        spot = lax.broadcasted_iota(jnp.int32, (width, F), 0)
        hot_left = jnp.where(spot == left_ref[...], 1.0, 0.0)
        hot_right = jnp.where(spot == right_ref[...], 1.0, 0.0)
        on_face = jnp.sum(hot_left, axis=1, keepdims=True)
        off_face = jnp.broadcast_to(1.0 - on_face, (width, 128)).astype(bf16)
        before = mm(jnp.where(col < row, 1.0, 0.0).astype(bf16), off_face)[:, :1]
        rest = jnp.where(col == F + before.astype(jnp.int32), 1.0 - on_face, 0.0)
        perm_t = rest + lanes(hot_left, jnp.zeros((width, width - F), f32))
        perm_t_ref[...] = perm_t.astype(bf16)
        perm_ref[...] = perm_t.T.astype(bf16)
        order_ref[...] = mm(hot_left.T.astype(bf16), hot_right.astype(bf16)).astype(bf16)
        coup = coup_ref[...]
        lead_ref[...] = -0.5 * mm(left3(coup.T), right3v(coup))

    def hear_stage():
        pl.semaphore_wait(known_sem.at[0], 2)
        tell(1)

    def second_stage():
        pl.semaphore_wait(known_sem.at[1], 2)
        tell(2)
        give_coupling.wait()
        following = next_ref[...]
        high, low = split(following)
        lowest = (following - high.astype(f32) - low.astype(f32)).astype(bf16)
        order = order_ref[...]
        here = mm(lanes(order, order, order), rows(high, low, lowest))
        d_all[slab] = here
        ends_ref[...] = here.T

    def spread_stage():
        pl.semaphore_wait(known_sem.at[2], 2)
        for t in range(slabs):
            @pl.when(d_goes(t))
            def _():
                give_d[t].start()

    def third_stage():
        def arrived(t, carry):
            remote(d_all.at[t], d_all.at[t], spread_sem.at[1, 0], d_sem.at[t], slab=slab).wait_recv()
            return carry

        lax.fori_loop(slab + 1, last - 1, arrived, 0)

        @pl.when(slab == last)
        def _():
            arrived(last - 1, 0)
            ends_ref[...] = d_all[last - 1]

    def finish(first, depth):
        piece_rows = pl.ds(first, depth)
        imag = first >= width
        there = pl.ds(first - width if imag else first, depth)
        diagonal = jnp.where(
            lax.broadcasted_iota(jnp.int32, (depth, width), 0) + (first - width if imag else first)
            == lax.broadcasted_iota(jnp.int32, (depth, width), 1),
            1.0, 0.0,
        )
        sigma = profile_ref[there, :] * acc[piece_rows, :]
        if imag:
            acc[piece_rows, :] = BROAD * diagonal - sigma
        else:
            acc[piece_rows, :] = energy_ref[0] * diagonal - ham_ref[there, :] - sigma

    settle = exchange(lines, green_in, green_ref, table_ref, got, part_send, part_recv, line_send, line_recv, acc,
                      piece_send, piece_recv, table_send, table_recv,
                      (first_stage, hear_stage, second_stage, spread_stage, third_stage), finish)

    perm = perm_ref[...]
    pieces = split(acc[:width, :]) + split(acc[width:, :])
    turned = mmt(rows(*pieces), perm).astype(bf16)
    placed = mm(perm, lanes(*[turned[k * width:(k + 1) * width] for k in range(4)]))
    a_real = placed[:, :width] + placed[:, width:2 * width]
    a_imag = placed[:, 2 * width:3 * width] + placed[:, 3 * width:]
    a_ref[:, :width] = a_real
    a_ref[:, width:] = a_imag
    inner = (row < F) & (col < F)
    modulus = jnp.where(inner, 0.0, jnp.sqrt(a_real * a_real + a_imag * a_imag))
    row_sums = jnp.sum(modulus, axis=1, keepdims=True)
    col_sums = jnp.sum(modulus, axis=0, keepdims=True)
    pa_ref[...] = lanes(a_real[:, :F], a_imag[:, :F])
    open_real = jnp.where(inner, 0.0, a_real)
    open_imag = jnp.where(inner, 0.0, a_imag)
    rh, rl = split(open_real)
    ih, il = split(open_imag)
    left = rows(lanes(rh, rh, rl, ih, ih, il), lanes(ih, ih, il, -rh, -rh, -rl))
    sk_ref[...] = mmt(left, lanes(rh, rl, rh, ih, il, ih))

    @pl.when(slab == 0)
    def _():
        b_ref[...] = lanes(jnp.zeros((F, F), f32), lead_ref[...])

    @pl.when(slab > 0)
    def _():
        forward.wait_recv()

    face = pa_ref[:F, :] - b_ref[...]
    pa_ref[:F, :] = face
    square = face * face
    face_mod = jnp.sqrt(square[:, :F] + square[:, F:])
    face_rows = jnp.sum(face_mod, axis=1, keepdims=True) + row_sums[:F]
    face_cols = jnp.sum(face_mod, axis=0, keepdims=True) + col_sums[:, :F]
    row_norm = jnp.maximum(jnp.max(row_sums[F:], axis=0, keepdims=True), jnp.max(face_rows, axis=0, keepdims=True))
    col_norm = jnp.maximum(jnp.max(col_sums[:, F:], axis=1, keepdims=True), jnp.max(face_cols, axis=1, keepdims=True))
    scale = 1.0 / (row_norm * col_norm)
    pa = pa_ref[...]
    other = swapped(face, 1.0, -1.0)
    ends = ends_ref[...]
    first = rows(face, other, lanes(ends, zero), lanes(zero, -ends))
    over = mmt(left3(first), right3(pa))
    down = mmt(left3(pa), right3(rows(face, -other)))
    inside = lax.broadcasted_iota(jnp.int32, (width, 2 * F), 1) < F
    below = (lax.broadcasted_iota(jnp.int32, (width, 2 * F), 0) >= F) & inside
    for part in range(2):
        base = part * width
        sk_ref[base:base + F, :] += over[part * F:(part + 1) * F]
        column = down if part == 0 else lanes(down[:, F:], down[:, :F])
        sk_ref[base:base + width, :2 * F] += jnp.where(below, column, 0.0)
    sym = unit - scale * sk_ref[:width, :]
    skew = -scale * sk_ref[width:, :]
    lr = scale * over[2 * F:3 * F]
    li = scale * over[3 * F:]

    def thin(level, real, imag):
        put(thin_ref.at[0], rows(real, imag))
        put(thin_ref.at[1], rows(-imag, real))
        product = mm(
            lanes(tripled(thin_ref.at[0]), tripled(thin_ref.at[1])), as_weights(s_ref.at[level], k_ref.at[level])
        )
        return product * (1.0 / FACTORS[level])

    grown, flipped = sym + skew, sym - skew
    for level in range(3):
        put(s_ref.at[level], sym)
        put(k_ref.at[level], skew)
        put(g_ref.at[level], grown)
        put(t_ref.at[level], flipped)
        grown = by_halves(
            lanes(tripled(g_ref.at[level]), tripled(t_ref.at[level])), as_weights(s_ref.at[level], k_ref.at[level])
        )
        result = thin(level, lr, li)
        lr = lr + result[:F]
        li = li + result[F:]
        flipped = grown.T
        sym = grown + flipped
        skew = grown - flipped
    put(s_ref.at[3], sym)
    put(k_ref.at[3], skew)
    ur, ui = sym[:F] * (1.0 / FACTORS[3]), skew[:F] * (1.0 / FACTORS[3])
    upper = mm(
        lanes(left3(rows(ur, ui)), left3(rows(-ui, ur))), as_weights(s_ref.at[3], k_ref.at[3])
    ) * (1.0 / FACTORS[3])
    result = rows(thin(3, lr, li), upper)
    w1r, w1i = ur + unit[:F], ui
    w2r, w2i = ur + result[2 * F:3 * F], ui + result[3 * F:]
    left = left3(lanes(lr, li, result[:F], result[F:2 * F]))
    right = right3(rows(lanes(w1r, w1i, w2r, w2i), lanes(-w1i, w1r, -w2i, w2r)))
    packed = mmt(left, right)
    both = rows(lanes(ends, zero), lanes(zero, ends))
    packed = mmt(left3(packed), right3(both))

    send_ref[...] = packed

    @pl.when(slab < last)
    def _():
        forward.start()

    @pl.when(slab == last)
    def _():
        for t in (3, 2, 4, 1, 5, 0, 6):
            messages[t].start()

    put(g_ref.at[3], grown)
    put(t_ref.at[3], flipped)
    part_g = g_ref[0, 0].astype(f32) + g_ref[0, 1].astype(f32) + unit
    part_t = t_ref[0, 0].astype(f32) + t_ref[0, 1].astype(f32) + unit
    for level in range(1, 4):
        part_g = part_g + by_halves(lanes(left3(part_g), left3(part_t)), as_weights(s_ref.at[level], k_ref.at[level])) * (
            1.0 / FACTORS[level]
        )
        part_t = part_g.T
    grown = by_halves(lanes(tripled(g_ref.at[3]), tripled(t_ref.at[3])), as_weights(s_ref.at[3], k_ref.at[3]))
    flipped = grown.T
    half = 0.5 * FACTORS[1] / (FACTORS[3] * FACTORS[3])
    highest = rows(right3v(half * (grown + flipped)), right3v(half * (grown - flipped)))
    part_g = part_g + by_halves(lanes(left3(part_g), left3(part_t)), highest)
    part_t = part_g.T
    pr = 0.5 * (part_g + part_t)
    pi = 0.5 * (part_g - part_t)
    a_ref[:F, :F] = face[:, :F]
    a_ref[:F, width:width + F] = face[:, F:]
    left = lanes(left3(a_ref[:, :width].T), left3(a_ref[:, width:].T))
    right = rows(right3v(lanes(pr, pi)), right3v(lanes(pi, -pr)))
    block = scale * mm(left, right)
    block_face = lanes(block[:F, :F], block[:F, width:width + F])
    face_all[slab] = block_face
    for t in (2, 1, 3, 0, 4, 5):
        @pl.when(face_goes(t))
        def _():
            give_face[t].start()

    hr, qr = split(block[:, :width])
    hi, qi = split(block[:, width:])
    turned = mm(perm_t_ref[...], lanes(hr, qr, hi, qi))
    back = turned.astype(bf16)
    back = mm(rows(*[back[:, k * width:(k + 1) * width] for k in range(4)]), perm)
    x_ref[0] = back[:width] + back[width:2 * width]
    x_ref[1] = back[2 * width:3 * width] + back[3 * width:]

    @pl.when(slab == last)
    def _():
        out_ref[0, 0, :, :, :] = x_ref[...]

    @pl.when(slab < last)
    def _():
        column = left3(
            lanes(
                turned[:, :F] + turned[:, width:width + F],
                turned[:, 2 * width:2 * width + F] + turned[:, 3 * width:3 * width + F],
            )
        )
        face_rows = mm(rows(hr[:F], qr[:F], hi[:F], qi[:F]), perm)
        rr = face_rows[:F] + face_rows[F:2 * F]
        ri = face_rows[2 * F:3 * F] + face_rows[3 * F:]
        across = across_of(rr, ri)
        one = unit[:F, :2 * F]
        part_ref[0] = jnp.zeros((F, 2 * F), f32)
        part_ref[1] = one
        part_ref[2] = one

        def compose(t, carry):
            remote(face_all.at[t], face_all.at[t], spread_sem.at[2, 0], face_sem.at[t], slab=slab).wait_recv()
            g = face_all[t]
            d = d_all[t - 1]
            both = right3(rows(lanes(d, zero), lanes(zero, d)))
            u = mm(left3(d), right3v(g))
            v = mmt(left3(g), both)
            k = mmt(left3(u), both)
            before, behind = part_ref[1], right3v(as_right(part_ref[2]))
            before = left3(before)
            part_ref[0] += mm(left3(mm(before, right3v(as_right(k)))), behind)
            part_ref[1] = mm(before, right3v(as_right(u)))
            part_ref[2] = mm(left3(v), behind)
            return carry

        lax.fori_loop(slab + 1, last, compose, 0)
        wide = mm(column, lanes(right3v(as_right(part_ref[0])), right3v(as_right(part_ref[1]))))
        more = mm(left3(wide[:, :2 * F]), across)
        x_ref[0] += more[:, :width]
        x_ref[1] += more[:, width:]
        column = left3(wide[:, 2 * F:])
        across = mm(left3(part_ref[2]), across_of(rr, ri))
        rr, ri = across[:, :width], across[:, width:]
        across = across_of(rr, ri)
        messages[0].wait_recv()
        incoming = right3v(as_right(m_ref[...]))
        more = mm(left3(mm(column, incoming)), across)
        out_ref[0, 0, 0, :, :] = x_ref[0] + more[:, :width]
        out_ref[0, 0, 1, :, :] = x_ref[1] + more[:, width:]

    @pl.when(slab < last)
    def _():
        forward.wait_send()

    @pl.when(slab == last)
    def _():
        for t in range(last):
            messages[t].wait_send()

    for t in range(slabs):
        @pl.when(d_goes(t))
        def _():
            give_d[t].wait_send()

        if t < last:
            @pl.when(face_goes(t))
            def _():
                give_face[t].wait_send()

    settle()


def run(energies, hamiltonian, coupling, green_prev, profile, phonon_weights, source, weight_index, left, right):
    width, faces = hamiltonian.shape[-1], coupling.shape[-1]
    slabs, lines = lax.axis_size("slab"), lax.axis_size("energy") // (NX * CORES)
    vmem, smem = pl.BlockSpec(memory_space=pltpu.VMEM), pl.BlockSpec(memory_space=pltpu.SMEM)
    face_block = pltpu.VMEM((faces, faces), f32)
    face_pair = pltpu.VMEM((faces, 2 * faces), f32)
    return pl.pallas_call(
        functools.partial(born_kernel, lines, slabs, width, faces),
        out_shape=jax.ShapeDtypeStruct((1, 1, 2, width, width), f32),
        in_specs=[smem] * 4 + [pl.BlockSpec(memory_space=pltpu.HBM)] * 6,
        out_specs=vmem,
        scratch_shapes=[
            pltpu.VMEM((2 * width, width), f32),
            pltpu.VMEM((width, width), f32),
            pltpu.VMEM((width, width), f32),
            face_block,
            pltpu.VMEM((1, faces), jnp.int32),
            pltpu.VMEM((1, faces), jnp.int32),
            pltpu.SemaphoreType.DMA((6,)),
        ] + EXCHANGE_SCRATCH(width) + [
            pltpu.VMEM((width, width), bf16),
            pltpu.VMEM((width, width), bf16),
            face_block,
            pltpu.VMEM((faces, faces), bf16),
            pltpu.VMEM((slabs, faces, faces), f32),
            pltpu.VMEM((slabs, faces, 2 * faces), f32),
            face_block, face_block,
            pltpu.VMEM((2 * width, width), f32),
            pltpu.VMEM((4, 2, width, width), bf16),
            pltpu.VMEM((4, 2, width, width), bf16),
            pltpu.VMEM((4, 2, width, width), bf16),
            pltpu.VMEM((4, 2, width, width), bf16),
            pltpu.VMEM((2, 2, 2 * faces, width), bf16),
            pltpu.VMEM((width, 2 * width), f32),
            face_pair, face_pair, face_pair,
            pltpu.VMEM((3, faces, 2 * faces), f32),
            pltpu.VMEM((width, 2 * faces), f32),
            pltpu.VMEM((2, width, width), f32),
            pltpu.SemaphoreType.DMA((2,)),
            pltpu.SemaphoreType.DMA((3,)),
            pltpu.SemaphoreType.DMA((3, slabs)),
            pltpu.SemaphoreType.DMA((slabs,)),
            pltpu.SemaphoreType.DMA((slabs,)),
            pltpu.SemaphoreType.REGULAR((3,)),
        ],
        compiler_params=pltpu.CompilerParams(
            collective_id=0, has_side_effects=True, vmem_limit_bytes=67043328
        ),
        name="born",
    )(
        energies, source, weight_index, phonon_weights,
        green_prev.reshape(2 * width, width), hamiltonian[0], profile, coupling[0], left, right,
    )


def solution(mesh):
    in_specs = (
        P("energy"),
        P("slab", None, None),
        P("slab", None, None),
        P("energy", "slab", None, None, None),
        P(),
        P(),
        P("energy", None),
        P("energy", None),
        P("slab", None),
        P("slab", None),
    )
    out_specs = P("energy", "slab", None, None, None)
    return jax.shard_map(run, mesh=mesh, in_specs=in_specs, out_specs=out_specs, check_vma=False)
```

```python
import functools
import jax
import jax.numpy as jnp
from jax import lax
from jax.experimental import pallas as pl
from jax.experimental.pallas import tpu as pltpu
from jax.sharding import PartitionSpec as P

BROAD = 0.02
f32 = jnp.float32
bf16 = jnp.bfloat16
MESH = pl.DeviceIdType.MESH


def mm(left, right):
    return jnp.dot(left, right, preferred_element_type=f32)


def mmt(left, right):
    return lax.dot_general(left, right, (((1,), (1,)), ((), ())), preferred_element_type=f32)


def by_halves(left, right):
    half = left.shape[0] // 2
    return rows(mm(left[:half], right), mm(left[half:], right))


def split(value):
    high = value.astype(bf16)
    return high, (value - high.astype(f32)).astype(bf16)


def lanes(*pieces):
    return jnp.concatenate(pieces, axis=1)


def rows(*pieces):
    return jnp.concatenate(pieces, axis=0)


def left3(value):
    high, low = split(value)
    return lanes(high, high, low)


def right3(value):
    high, low = split(value)
    return lanes(high, low, high)


def right3v(value):
    high, low = split(value)
    return rows(high, low, high)


def swapped(packed, low_sign, high_sign):
    half = packed.shape[1] // 2
    lane = lax.broadcasted_iota(jnp.int32, packed.shape, 1)
    turned = lanes(packed[:, half:], packed[:, :half])
    return jnp.where(lane < half, low_sign * turned, high_sign * turned)


def put(ref, value):
    high, low = split(value)
    ref[0] = high
    ref[1] = low


def tripled(ref):
    return lanes(ref[0], ref[0], ref[1])


def as_weights(sym_ref, skew_ref):
    return rows(sym_ref[0], sym_ref[1], sym_ref[0], skew_ref[0], skew_ref[1], skew_ref[0])


def across_of(real, imag):
    return right3v(rows(lanes(real, imag), lanes(-imag, real)))


def as_right(packed):
    return rows(packed, swapped(packed, -1.0, 1.0))


NX = 4
CORES = 2
DEPTHS = (64,) * 8
CHUNKS = len(DEPTHS)
AHEAD = 3
FAR_LAG = 2
PARTNER_LAG = 2
LINE_LAG = 5
MEANWHILE = (1, 2, 3, 6)
FACTORS = (1.0, 2.0, 4.0, 16.0)
TABLE = 32


def where_on_energy():
    spot = lax.axis_index("energy")
    core = lax.rem(spot, CORES)
    chip = lax.div(spot, CORES)
    return lax.rem(chip, NX), lax.div(chip, NX), core


def energy_of(x, z, core):
    return (z * NX + x) * CORES + core


def remote(source, target, send, recv, **device):
    return pltpu.make_async_remote_copy(
        src_ref=source, dst_ref=target, send_sem=send, recv_sem=recv, device_id=device, device_id_type=MESH
    )


def greet(lines, slabs):
    x, z, core = where_on_energy()
    barrier = pltpu.get_barrier_semaphore()

    def signal(**device):
        pl.semaphore_signal(barrier, inc=1, device_id=device, device_id_type=MESH)

    signal(energy=energy_of(lax.rem(x + 1, NX), z, core))
    signal(energy=energy_of(lax.rem(x + NX - 1, NX), z, core))
    signal(energy=energy_of(x, z, 1 - core))
    count = 3
    for step, there in ((1, z < lines - 1), (-1, z > 0)):
        @pl.when(there)
        def _():
            signal(energy=energy_of(x, z + step, core))
            signal(energy=energy_of(x, z + step, 1 - core))
        count = count + 2 * there.astype(jnp.int32)
    if slabs > 1:
        slab = lax.axis_index("slab")
        for step in (1, slabs - 1):
            signal(slab=lax.rem(slab + step, slabs))
        count = count + 2
    return barrier, count


def make_table(source_ref, index_ref, weights_ref, table_ref):
    here = lax.axis_index("energy")
    row = lax.broadcasted_iota(jnp.int32, (TABLE, 128), 0)
    total = jnp.zeros((TABLE, 128), f32)
    for term in range(2):
        weight = weights_ref[index_ref[0, term]]
        distance = source_ref[0, term] - here + TABLE // 2
        total = total + jnp.where(row == distance, weight, 0.0)
    table_ref[0] = total


def exchange(lines, green, own, table_ref, got, part_send, part_recv, line_send, line_recv, acc,
             send_sem, recv_sem, table_send, table_recv, meanwhile, finish):
    x, z, core = where_on_energy()
    starts = [sum(DEPTHS[:q]) for q in range(CHUNKS)]
    right = energy_of(lax.rem(x + 1, NX), z, core)
    left = energy_of(lax.rem(x + NX - 1, NX), z, core)
    partner = energy_of(x, z, 1 - core)
    up_there, down_there = z < lines - 1, z > 0
    up, down = energy_of(x, z + 1, core), energy_of(x, z - 1, core)
    up_other, down_other = energy_of(x, z + 1, 1 - core), energy_of(x, z - 1, 1 - core)

    def span(chunk):
        return pl.ds(starts[chunk], DEPTHS[chunk])

    def part(ref, chunk):
        return ref.at[span(chunk), :]

    def tables(flow, device):
        return remote(table_ref.at[0], table_ref.at[flow + 1], table_send.at[flow], table_recv.at[flow], energy=device)

    to_partner = tables(0, partner)
    to_up, to_up_other = tables(3, up), tables(4, up_other)
    to_down, to_down_other = tables(1, down), tables(2, down_other)

    def piece(flow, chunk, source, target, device):
        return remote(source, target, send_sem.at[flow, chunk], recv_sem.at[flow, chunk], energy=device)

    to_right = [piece(0, q, part(green, q), part(got.at[0], q), right) for q in range(CHUNKS)]
    to_left = [piece(1, q, part(green, q), part(got.at[1], q), left) for q in range(CHUNKS)]
    onward = [
        piece(2, q, part(got.at[q % 2], q), part(got.at[2], q), right if q % 2 == 0 else left)
        for q in range(CHUNKS)
    ]
    across = [
        [piece(3 + k, q, part(part_send.at[k], q), part(part_recv.at[k], q), partner) for q in range(CHUNKS)]
        for k in range(3)
    ]
    upward = [piece(6, q, part(line_send.at[0], q), part(line_recv.at[0], q), up) for q in range(CHUNKS)]
    downward = [piece(7, q, part(line_send.at[1], q), part(line_recv.at[1], q), down) for q in range(CHUNKS)]

    def own_start(chunk):
        to_right[chunk].start()
        to_left[chunk].start()

    for chunk in range(AHEAD):
        own_start(chunk)
    to_partner.start()

    @pl.when(up_there)
    def _():
        to_up.start()
        to_up_other.start()

    @pl.when(down_there)
    def _():
        to_down.start()
        to_down_other.start()

    meanwhile[0]()
    to_partner.wait()

    @pl.when(up_there)
    def _():
        to_up.wait_send()
        to_up_other.wait_send()
        to_down.wait_recv()
        to_down_other.wait_recv()

    @pl.when(down_there)
    def _():
        to_down.wait_send()
        to_down_other.wait_send()
        to_up.wait_recv()
        to_up_other.wait_recv()

    apart = [0] + [lax.rem(x + step, NX) - x for step in (3, 1, 2)]

    def weighted(slot, line, other, chunk):
        total = None
        for k in range(4):
            lag = 2 * apart[k] + (2 * core - 1 if other else 0) - 8 * line + TABLE // 2
            weight = table_ref[slot, pl.ds(lag, 1), :]
            block = (own if k == 0 else got.at[k - 1])[span(chunk), :]
            term = lanes(weight, weight) * block
            total = term if total is None else total + term
        return total

    for step in range(CHUNKS + LINE_LAG):
        q = step
        if q < CHUNKS:
            to_right[q].wait_recv()
            to_left[q].wait_recv()
            onward[q].start()
            if q + AHEAD < CHUNKS:
                own_start(q + AHEAD)
        if step in MEANWHILE:
            meanwhile[1 + MEANWHILE.index(step)]()
        q = step - FAR_LAG
        if 0 <= q < CHUNKS:
            onward[q].wait_recv()
            piece_rows = span(q)
            acc[piece_rows, :] = weighted(0, 0, False, q)
            part_send[0, piece_rows, :] = weighted(1, 0, True, q)
            across[0][q].start()

            @pl.when(up_there)
            def _():
                line_send[0, piece_rows, :] = weighted(2, 1, False, q)
                part_send[1, piece_rows, :] = weighted(3, 1, True, q)
                across[1][q].start()

            @pl.when(down_there)
            def _():
                line_send[1, piece_rows, :] = weighted(4, -1, False, q)
                part_send[2, piece_rows, :] = weighted(5, -1, True, q)
                across[2][q].start()
        q = step - PARTNER_LAG
        if 0 <= q < CHUNKS:
            piece_rows = span(q)
            across[0][q].wait_recv()
            acc[piece_rows, :] += part_recv[0, piece_rows, :]

            @pl.when(up_there)
            def _():
                across[1][q].wait_recv()
                line_send[0, piece_rows, :] += part_recv[1, piece_rows, :]
                upward[q].start()

            @pl.when(down_there)
            def _():
                across[2][q].wait_recv()
                line_send[1, piece_rows, :] += part_recv[2, piece_rows, :]
                downward[q].start()
        q = step - LINE_LAG
        if 0 <= q < CHUNKS:
            piece_rows = span(q)

            @pl.when(down_there)
            def _():
                upward[q].wait_recv()
                acc[piece_rows, :] += line_recv[0, piece_rows, :]

            @pl.when(up_there)
            def _():
                downward[q].wait_recv()
                acc[piece_rows, :] += line_recv[1, piece_rows, :]

            finish(starts[q], DEPTHS[q])

    def settle():
        for q in range(CHUNKS):
            to_right[q].wait_send()
            to_left[q].wait_send()
            onward[q].wait_send()
            across[0][q].wait_send()

            @pl.when(up_there)
            def _():
                across[1][q].wait_send()
                upward[q].wait_send()

            @pl.when(down_there)
            def _():
                across[2][q].wait_send()
                downward[q].wait_send()

    return settle


EXCHANGE_SCRATCH = lambda width: [
    pltpu.VMEM((6, TABLE, 128), f32),
    pltpu.VMEM((3, 2 * width, width), f32),
    pltpu.VMEM((3, 2 * width, width), f32),
    pltpu.VMEM((3, 2 * width, width), f32),
    pltpu.VMEM((2, 2 * width, width), f32),
    pltpu.VMEM((2, 2 * width, width), f32),
    pltpu.VMEM((2 * width, width), f32),
    pltpu.SemaphoreType.DMA((8, CHUNKS)),
    pltpu.SemaphoreType.DMA((8, CHUNKS)),
    pltpu.SemaphoreType.DMA((5,)),
    pltpu.SemaphoreType.DMA((5,)),
]


def born_kernel(
    lines, slabs, width, faces,
    energy_ref, source_ref, index_ref, weights_ref, green_in, ham_in, profile_in, coup_in, left_in, right_in,
    out_ref,
    green_ref, ham_ref, profile_ref, coup_ref, left_ref, right_ref, load_sem,
    table_ref, got, part_send, part_recv, line_send, line_recv, acc, piece_send, piece_recv, table_send, table_recv,
    perm_ref, perm_t_ref, next_ref, order_ref, d_all, face_all, ends_ref, lead_ref,
    sk_ref, g_ref, t_ref, s_ref, k_ref, thin_ref, a_ref, b_ref, m_ref, send_ref, part_ref, pa_ref, x_ref,
    send_sem, recv_sem, spread_sem, d_sem, face_sem, known_sem,
):
    slab = lax.axis_index("slab")
    F = faces
    row = lax.broadcasted_iota(jnp.int32, (width, width), 0)
    col = lax.broadcasted_iota(jnp.int32, (width, width), 1)
    unit = jnp.where(row == col, 1.0, 0.0)
    barrier, greetings = greet(lines, slabs)
    loads = [
        pltpu.make_async_copy(source, target, load_sem.at[k])
        for k, (source, target) in enumerate((
            (coup_in, coup_ref), (left_in, left_ref), (right_in, right_ref),
            (green_in, green_ref), (ham_in, ham_ref), (profile_in, profile_ref),
        ))
    ]
    for load in loads:
        load.start()
    make_table(source_ref, index_ref, weights_ref, table_ref)
    pl.semaphore_wait(barrier, greetings)
    last = slabs - 1
    forward = remote(send_ref, b_ref, send_sem.at[0], recv_sem.at[0], slab=lax.rem(slab + 1, slabs))
    give_coupling = remote(coup_ref, next_ref, send_sem.at[1], recv_sem.at[1], slab=lax.rem(slab + last, slabs))
    messages = [remote(send_ref, m_ref, spread_sem.at[0, t], recv_sem.at[2], slab=t) for t in range(last)]
    give_d = [
        remote(d_all.at[slab], d_all.at[slab], spread_sem.at[1, t], d_sem.at[slab], slab=t) for t in range(slabs)
    ]
    give_face = [
        remote(face_all.at[slab], face_all.at[slab], spread_sem.at[2, t], face_sem.at[slab], slab=t)
        for t in range(last)
    ]

    def d_goes(t):
        return (slab == last - 1) if t == last else ((slab > t) & (slab < last - 1))

    def face_goes(t):
        return (slab > t) & (slab < last)

    zero = jnp.zeros((F, F), f32)

    def tell(hop):
        for step in (1, last):
            pl.semaphore_signal(
                known_sem.at[hop], inc=1, device_id={"slab": lax.rem(slab + step, slabs)}, device_id_type=MESH
            )

    def first_stage():
        tell(0)
        for load in loads:
            load.wait()
        give_coupling.start()
        spot = lax.broadcasted_iota(jnp.int32, (width, F), 0)
        hot_left = jnp.where(spot == left_ref[...], 1.0, 0.0)
        hot_right = jnp.where(spot == right_ref[...], 1.0, 0.0)
        on_face = jnp.sum(hot_left, axis=1, keepdims=True)
        off_face = jnp.broadcast_to(1.0 - on_face, (width, 128)).astype(bf16)
        before = mm(jnp.where(col < row, 1.0, 0.0).astype(bf16), off_face)[:, :1]
        rest = jnp.where(col == F + before.astype(jnp.int32), 1.0 - on_face, 0.0)
        perm_t = rest + lanes(hot_left, jnp.zeros((width, width - F), f32))
        perm_t_ref[...] = perm_t.astype(bf16)
        perm_ref[...] = perm_t.T.astype(bf16)
        order_ref[...] = mm(hot_left.T.astype(bf16), hot_right.astype(bf16)).astype(bf16)
        coup = coup_ref[...]
        lead_ref[...] = -0.5 * mm(left3(coup.T), right3v(coup))

    def hear_stage():
        pl.semaphore_wait(known_sem.at[0], 2)
        tell(1)

    def second_stage():
        pl.semaphore_wait(known_sem.at[1], 2)
        tell(2)
        give_coupling.wait()
        following = next_ref[...]
        high, low = split(following)
        lowest = (following - high.astype(f32) - low.astype(f32)).astype(bf16)
        order = order_ref[...]
        here = mm(lanes(order, order, order), rows(high, low, lowest))
        d_all[slab] = here
        ends_ref[...] = here.T

    def spread_stage():
        pl.semaphore_wait(known_sem.at[2], 2)
        for t in range(slabs):
            @pl.when(d_goes(t))
            def _():
                give_d[t].start()

    def third_stage():
        def arrived(t, carry):
            remote(d_all.at[t], d_all.at[t], spread_sem.at[1, 0], d_sem.at[t], slab=slab).wait_recv()
            return carry

        lax.fori_loop(slab + 1, last - 1, arrived, 0)

        @pl.when(slab == last)
        def _():
            arrived(last - 1, 0)
            ends_ref[...] = d_all[last - 1]

    def finish(first, depth):
        piece_rows = pl.ds(first, depth)
        imag = first >= width
        there = pl.ds(first - width if imag else first, depth)
        diagonal = jnp.where(
            lax.broadcasted_iota(jnp.int32, (depth, width), 0) + (first - width if imag else first)
            == lax.broadcasted_iota(jnp.int32, (depth, width), 1),
            1.0, 0.0,
        )
        sigma = profile_ref[there, :] * acc[piece_rows, :]
        if imag:
            acc[piece_rows, :] = BROAD * diagonal - sigma
        else:
            acc[piece_rows, :] = energy_ref[0] * diagonal - ham_ref[there, :] - sigma

    settle = exchange(lines, green_in, green_ref, table_ref, got, part_send, part_recv, line_send, line_recv, acc,
                      piece_send, piece_recv, table_send, table_recv,
                      (first_stage, hear_stage, second_stage, spread_stage, third_stage), finish)

    perm = perm_ref[...]
    pieces = split(acc[:width, :]) + split(acc[width:, :])
    turned = mmt(rows(*pieces), perm).astype(bf16)
    placed = mm(perm, lanes(*[turned[k * width:(k + 1) * width] for k in range(4)]))
    a_real = placed[:, :width] + placed[:, width:2 * width]
    a_imag = placed[:, 2 * width:3 * width] + placed[:, 3 * width:]
    a_ref[:, :width] = a_real
    a_ref[:, width:] = a_imag
    inner = (row < F) & (col < F)
    modulus = jnp.where(inner, 0.0, jnp.sqrt(a_real * a_real + a_imag * a_imag))
    row_sums = jnp.sum(modulus, axis=1, keepdims=True)
    col_sums = jnp.sum(modulus, axis=0, keepdims=True)
    pa_ref[...] = lanes(a_real[:, :F], a_imag[:, :F])
    open_real = jnp.where(inner, 0.0, a_real)
    open_imag = jnp.where(inner, 0.0, a_imag)
    rh, rl = split(open_real)
    ih, il = split(open_imag)
    left = rows(lanes(rh, rh, rl, ih, ih, il), lanes(ih, ih, il, -rh, -rh, -rl))
    right = lanes(rh, rl, rh, ih, il, ih)
    sk_ref[:width, :] = mmt(left[:width], right)
    sk_ref[width:, :] = mmt(left[width:], right)

    @pl.when(slab == 0)
    def _():
        b_ref[...] = lanes(jnp.zeros((F, F), f32), lead_ref[...])

    @pl.when(slab > 0)
    def _():
        forward.wait_recv()

    face = pa_ref[:F, :] - b_ref[...]
    pa_ref[:F, :] = face
    square = face * face
    face_mod = jnp.sqrt(square[:, :F] + square[:, F:])
    face_rows = jnp.sum(face_mod, axis=1, keepdims=True) + row_sums[:F]
    face_cols = jnp.sum(face_mod, axis=0, keepdims=True) + col_sums[:, :F]
    row_norm = jnp.maximum(jnp.max(row_sums[F:], axis=0, keepdims=True), jnp.max(face_rows, axis=0, keepdims=True))
    col_norm = jnp.maximum(jnp.max(col_sums[:, F:], axis=1, keepdims=True), jnp.max(face_cols, axis=1, keepdims=True))
    scale = 1.0 / (row_norm * col_norm)
    pa = pa_ref[...]
    other = swapped(face, 1.0, -1.0)
    ends = ends_ref[...]
    first = rows(face, other, lanes(ends, zero), lanes(zero, -ends))
    over = mmt(left3(first), right3(pa))
    down = mmt(left3(pa), right3(rows(face, -other)))
    inside = lax.broadcasted_iota(jnp.int32, (width, 2 * F), 1) < F
    below = (lax.broadcasted_iota(jnp.int32, (width, 2 * F), 0) >= F) & inside
    for part in range(2):
        base = part * width
        sk_ref[base:base + F, :] += over[part * F:(part + 1) * F]
        column = down if part == 0 else lanes(down[:, F:], down[:, :F])
        sk_ref[base:base + width, :2 * F] += jnp.where(below, column, 0.0)
    sym = unit - scale * sk_ref[:width, :]
    skew = -scale * sk_ref[width:, :]
    lr = scale * over[2 * F:3 * F]
    li = scale * over[3 * F:]

    def thin(level, real, imag):
        put(thin_ref.at[0], rows(real, imag))
        put(thin_ref.at[1], rows(-imag, real))
        product = mm(
            lanes(tripled(thin_ref.at[0]), tripled(thin_ref.at[1])), as_weights(s_ref.at[level], k_ref.at[level])
        )
        return product * (1.0 / FACTORS[level])

    grown, flipped = sym + skew, sym - skew
    for level in range(3):
        put(s_ref.at[level], sym)
        put(k_ref.at[level], skew)
        put(g_ref.at[level], grown)
        put(t_ref.at[level], flipped)
        grown = by_halves(
            lanes(tripled(g_ref.at[level]), tripled(t_ref.at[level])), as_weights(s_ref.at[level], k_ref.at[level])
        )
        result = thin(level, lr, li)
        lr = lr + result[:F]
        li = li + result[F:]
        flipped = grown.T
        sym = grown + flipped
        skew = grown - flipped
    put(s_ref.at[3], sym)
    put(k_ref.at[3], skew)
    ur, ui = sym[:F] * (1.0 / FACTORS[3]), skew[:F] * (1.0 / FACTORS[3])
    upper = mm(
        lanes(left3(rows(ur, ui)), left3(rows(-ui, ur))), as_weights(s_ref.at[3], k_ref.at[3])
    ) * (1.0 / FACTORS[3])
    result = rows(thin(3, lr, li), upper)
    w1r, w1i = ur + unit[:F], ui
    w2r, w2i = ur + result[2 * F:3 * F], ui + result[3 * F:]
    left = left3(lanes(lr, li, result[:F], result[F:2 * F]))
    right = right3(rows(lanes(w1r, w1i, w2r, w2i), lanes(-w1i, w1r, -w2i, w2r)))
    packed = mmt(left, right)
    both = rows(lanes(ends, zero), lanes(zero, ends))
    packed = mmt(left3(packed), right3(both))

    send_ref[...] = packed

    @pl.when(slab < last)
    def _():
        forward.start()

    @pl.when(slab == last)
    def _():
        for t in (3, 2, 4, 1, 5, 0, 6):
            messages[t].start()

    put(g_ref.at[3], grown)
    put(t_ref.at[3], flipped)
    part_g = g_ref[0, 0].astype(f32) + g_ref[0, 1].astype(f32) + unit
    part_t = t_ref[0, 0].astype(f32) + t_ref[0, 1].astype(f32) + unit
    for level in range(1, 4):
        part_g = part_g + by_halves(lanes(left3(part_g), left3(part_t)), as_weights(s_ref.at[level], k_ref.at[level])) * (
            1.0 / FACTORS[level]
        )
        part_t = part_g.T
    grown = by_halves(lanes(tripled(g_ref.at[3]), tripled(t_ref.at[3])), as_weights(s_ref.at[3], k_ref.at[3]))
    flipped = grown.T
    half = 0.5 * FACTORS[1] / (FACTORS[3] * FACTORS[3])
    highest = rows(right3v(half * (grown + flipped)), right3v(half * (grown - flipped)))
    part_g = part_g + by_halves(lanes(left3(part_g), left3(part_t)), highest)
    part_t = part_g.T
    pr = 0.5 * (part_g + part_t)
    pi = 0.5 * (part_g - part_t)
    a_ref[:F, :F] = face[:, :F]
    a_ref[:F, width:width + F] = face[:, F:]
    left = lanes(left3(a_ref[:, :width].T), left3(a_ref[:, width:].T))
    right = rows(right3v(lanes(pr, pi)), right3v(lanes(pi, -pr)))
    block = scale * mm(left, right)
    block_face = lanes(block[:F, :F], block[:F, width:width + F])
    face_all[slab] = block_face
    for t in (2, 1, 3, 0, 4, 5):
        @pl.when(face_goes(t))
        def _():
            give_face[t].start()

    hr, qr = split(block[:, :width])
    hi, qi = split(block[:, width:])
    turned = mm(perm_t_ref[...], lanes(hr, qr, hi, qi))
    back = turned.astype(bf16)
    back = mm(rows(*[back[:, k * width:(k + 1) * width] for k in range(4)]), perm)
    x_ref[0] = back[:width] + back[width:2 * width]
    x_ref[1] = back[2 * width:3 * width] + back[3 * width:]

    @pl.when(slab == last)
    def _():
        out_ref[0, 0, :, :, :] = x_ref[...]

    @pl.when(slab < last)
    def _():
        column = left3(
            lanes(
                turned[:, :F] + turned[:, width:width + F],
                turned[:, 2 * width:2 * width + F] + turned[:, 3 * width:3 * width + F],
            )
        )
        face_rows = mm(rows(hr[:F], qr[:F], hi[:F], qi[:F]), perm)
        rr = face_rows[:F] + face_rows[F:2 * F]
        ri = face_rows[2 * F:3 * F] + face_rows[3 * F:]
        across = across_of(rr, ri)
        one = unit[:F, :2 * F]
        part_ref[0] = jnp.zeros((F, 2 * F), f32)
        part_ref[1] = one
        part_ref[2] = one

        def compose(t, carry):
            remote(face_all.at[t], face_all.at[t], spread_sem.at[2, 0], face_sem.at[t], slab=slab).wait_recv()
            g = face_all[t]
            d = d_all[t - 1]
            both = right3(rows(lanes(d, zero), lanes(zero, d)))
            u = mm(left3(d), right3v(g))
            v = mmt(left3(g), both)
            k = mmt(left3(u), both)
            before, behind = part_ref[1], right3v(as_right(part_ref[2]))
            before = left3(before)
            part_ref[0] += mm(left3(mm(before, right3v(as_right(k)))), behind)
            part_ref[1] = mm(before, right3v(as_right(u)))
            part_ref[2] = mm(left3(v), behind)
            return carry

        lax.fori_loop(slab + 1, last, compose, 0)
        wide = mm(column, lanes(right3v(as_right(part_ref[0])), right3v(as_right(part_ref[1]))))
        more = mm(left3(wide[:, :2 * F]), across)
        x_ref[0] += more[:, :width]
        x_ref[1] += more[:, width:]
        column = left3(wide[:, 2 * F:])
        across = mm(left3(part_ref[2]), across_of(rr, ri))
        rr, ri = across[:, :width], across[:, width:]
        across = across_of(rr, ri)
        messages[0].wait_recv()
        incoming = right3v(as_right(m_ref[...]))
        more = mm(left3(mm(column, incoming)), across)
        out_ref[0, 0, 0, :, :] = x_ref[0] + more[:, :width]
        out_ref[0, 0, 1, :, :] = x_ref[1] + more[:, width:]

    @pl.when(slab < last)
    def _():
        forward.wait_send()

    @pl.when(slab == last)
    def _():
        for t in range(last):
            messages[t].wait_send()

    for t in range(slabs):
        @pl.when(d_goes(t))
        def _():
            give_d[t].wait_send()

        if t < last:
            @pl.when(face_goes(t))
            def _():
                give_face[t].wait_send()

    settle()


def run(energies, hamiltonian, coupling, green_prev, profile, phonon_weights, source, weight_index, left, right):
    width, faces = hamiltonian.shape[-1], coupling.shape[-1]
    slabs, lines = lax.axis_size("slab"), lax.axis_size("energy") // (NX * CORES)
    vmem, smem = pl.BlockSpec(memory_space=pltpu.VMEM), pl.BlockSpec(memory_space=pltpu.SMEM)
    face_block = pltpu.VMEM((faces, faces), f32)
    face_pair = pltpu.VMEM((faces, 2 * faces), f32)
    return pl.pallas_call(
        functools.partial(born_kernel, lines, slabs, width, faces),
        out_shape=jax.ShapeDtypeStruct((1, 1, 2, width, width), f32),
        in_specs=[smem] * 4 + [pl.BlockSpec(memory_space=pltpu.HBM)] * 6,
        out_specs=vmem,
        scratch_shapes=[
            pltpu.VMEM((2 * width, width), f32),
            pltpu.VMEM((width, width), f32),
            pltpu.VMEM((width, width), f32),
            face_block,
            pltpu.VMEM((1, faces), jnp.int32),
            pltpu.VMEM((1, faces), jnp.int32),
            pltpu.SemaphoreType.DMA((6,)),
        ] + EXCHANGE_SCRATCH(width) + [
            pltpu.VMEM((width, width), bf16),
            pltpu.VMEM((width, width), bf16),
            face_block,
            pltpu.VMEM((faces, faces), bf16),
            pltpu.VMEM((slabs, faces, faces), f32),
            pltpu.VMEM((slabs, faces, 2 * faces), f32),
            face_block, face_block,
            pltpu.VMEM((2 * width, width), f32),
            pltpu.VMEM((4, 2, width, width), bf16),
            pltpu.VMEM((4, 2, width, width), bf16),
            pltpu.VMEM((4, 2, width, width), bf16),
            pltpu.VMEM((4, 2, width, width), bf16),
            pltpu.VMEM((2, 2, 2 * faces, width), bf16),
            pltpu.VMEM((width, 2 * width), f32),
            face_pair, face_pair, face_pair,
            pltpu.VMEM((3, faces, 2 * faces), f32),
            pltpu.VMEM((width, 2 * faces), f32),
            pltpu.VMEM((2, width, width), f32),
            pltpu.SemaphoreType.DMA((2,)),
            pltpu.SemaphoreType.DMA((3,)),
            pltpu.SemaphoreType.DMA((3, slabs)),
            pltpu.SemaphoreType.DMA((slabs,)),
            pltpu.SemaphoreType.DMA((slabs,)),
            pltpu.SemaphoreType.REGULAR((3,)),
        ],
        compiler_params=pltpu.CompilerParams(
            collective_id=0, has_side_effects=True, vmem_limit_bytes=67043328
        ),
        name="born",
    )(
        energies, source, weight_index, phonon_weights,
        green_prev.reshape(2 * width, width), hamiltonian[0], profile, coupling[0], left, right,
    )


def solution(mesh):
    in_specs = (
        P("energy"),
        P("slab", None, None),
        P("slab", None, None),
        P("energy", "slab", None, None, None),
        P(),
        P(),
        P("energy", None),
        P("energy", None),
        P("slab", None),
        P("slab", None),
    )
    out_specs = P("energy", "slab", None, None, None)
    return jax.shard_map(run, mesh=mesh, in_specs=in_specs, out_specs=out_specs, check_vma=False)
```
